512 devices in a mesh: elem: 8 (over y_hi, x), band: 64 (over z, y_lo, core).
Axes of the slice: x: 4, y: 4 (y_hi: 2, y_lo: 2; y = y_hi * 2 + y_lo), z: 16, core: 2. Of those that a mesh axis runs over, the one named last changes fastest.
Arguments:
- start_bands: bfloat16 [2048, 6144], P('band', 'elem'), may hold values from -6 to 6
- hamiltonian: bfloat16 [32, 7, 192, 192], P('elem'), may hold values from -0.15625 to 0.15625
- neighbours: int32 [32, 6], P('elem'), may hold values from 0 to 3
- basis_count: int32 [32], P('elem'), may hold values from 128 to 192, as said below
- owner_rows: int32 [64], replicated, may hold values from 1 to 36, 768 in all
- rotation: bfloat16 [2048, 2048], P(None, 'band'), may hold values from -0.125 to 0.125
Outputs:
- filtered: bfloat16 [2048, 6144], P('band', 'elem')
- rotated: bfloat16 [18432, 2048], P(('elem', 'band'))
The draws below stay inside these ranges and needn't reach their ends.
Inputs may be any that keep to these rules, and one draw needn't show every extreme that they name: `basis_count`: each element holds 128 to 192 basis functions; some element holds exactly 192 and some exactly 128. `neighbours`: any position 0 to 3 may appear in any slot, the element's own position too. `owner_rows`: the entries sum to 768; the largest is exactly 36.
All inputs are finite; a program needn't handle non-finite values.
Results may differ from the reference program's by a relative error of at most 0.013.
Values may be sent and summed in bfloat16 or wider, within the bound.
No kernel may reach another device: no remote copies, remote signals or barrier semaphores. Data moves between devices by JAX's collectives and lax.ppermute only.
A program may use at most 64 MiB of HBM per device.

```python
import math
import jax
import jax.numpy as jnp
import numpy as np
from jax import lax

NB = 192
NBMIN = 128
BANDS = 2048
DEGREE = 8
GROUPS = 8
PLANES = 8
ELEMS = 32
ROWS = 6144
ROWS_GRP = 768
OWNERS = 64
CAP = 36


def draw_basis_count(key, part):
    key_counts, key_places = jax.random.split(jax.random.fold_in(key, 11))
    counts_drawn = jax.random.randint(key_counts, (ELEMS,), NBMIN, NB + 1, dtype=jnp.int32)
    positions = jax.random.permutation(key_places, ELEMS)
    counts_drawn = counts_drawn.at[positions[0]].set(NB)
    counts_drawn = counts_drawn.at[positions[1]].set(NBMIN)
    return counts_drawn


def with_ends(result, key, low, largest):
    place = [jax.random.randint(jax.random.fold_in(key, axis), (), 0, length) for axis, length in enumerate(result.shape)]
    main_axis = result.shape.index(max(result.shape))
    neighbour = place[:main_axis] + [(place[main_axis] + 1) % result.shape[main_axis]] + place[main_axis + 1:]
    return result.at[tuple(place)].set(low).at[tuple(neighbour)].set(largest)


def block_scale(own_key, extent, cuts, low, top_value):
    level, own = 1.0, jax.random.fold_in(own_key, 6)
    for position, blocks in cuts:
        heights = jnp.exp(jax.random.uniform(jax.random.fold_in(own, position), (blocks,), jnp.float32, low / len(cuts), top_value / len(cuts)))
        level = level * jnp.repeat(heights, extent[position] // blocks).reshape([-1 if axis == position else 1 for axis in range(len(extent))])
    return level


def split_up(number_of, total, limit, skew):
    weights = [(1 << 20) // math.isqrt(grade ** skew) + 1 for grade in range(2, number_of + 1)]
    spare, given = total - limit - (number_of - 1), [1] * (number_of - 1)
    while spare > 0:
        free = [i for i in range(number_of - 1) if given[i] < limit]
        pool, left = sum([weights[i] for i in free]), spare
        for i in free:
            more = min(limit - given[i], max(1, left * weights[i] // pool), spare)
            given[i] = given[i] + more
            spare = spare - more
    return np.array([limit] + given)


def ragged_sizes(stream_key, amount, total, most, skew):
    if amount == 2:
        one = jax.random.randint(stream_key, (), max(1, total - most), min(most, total - 1) + 1)
        return jnp.stack([one, total - one])
    tallies = jnp.asarray(split_up(amount, total, most, skew), jnp.int32)
    pairs = (amount - 1) // 2
    donor, taker = tallies[1:1 + 2 * pairs:2], tallies[2:2 + 2 * pairs:2]
    room = jnp.minimum(donor - 1, most - taker)
    passed = jax.random.randint(jax.random.fold_in(stream_key, 1), (pairs,), 0, 1 << 20) % (room + 1)
    tallies = tallies.at[1:1 + 2 * pairs:2].set(donor - passed).at[2:2 + 2 * pairs:2].set(taker + passed)
    return tallies[jax.random.permutation(jax.random.fold_in(stream_key, 2), amount)]


def noise(key, dims, width, limit, cuts=(), held_as=jnp.bfloat16):
    gain = block_scale(key, dims, cuts, -0.22, 0.18) if cuts else 1.0
    values = jax.random.normal(key, dims, jnp.float32) * width * gain
    return jnp.minimum(jnp.maximum(values, -limit), limit).astype(held_as)


def setup_inputs(seed: int = 0) -> dict:
    key_list = jax.random.split(jax.random.key(seed), 7)
    return {
        "start_bands": noise(key_list[0], (BANDS, ROWS), 1.0, 6.0, ((0, 64), (1, 8))),
        "hamiltonian": noise(key_list[1], (ELEMS, 7, NB, NB), (7 * NB) ** -0.5, 0.15625, ((0, 8),)),
        "neighbours": with_ends(jax.random.randint(key_list[2], (ELEMS, 6), 0, 4), jax.random.fold_in(key_list[2], 1), 0, 3).astype(jnp.int32),
        "basis_count": draw_basis_count(jax.random.fold_in(key_list[6], 71), 0),
        "owner_rows": ragged_sizes(key_list[4], OWNERS, ROWS_GRP, CAP, 2).astype(jnp.int32),
        "rotation": noise(key_list[5], (BANDS, BANDS), BANDS ** -0.5, 0.125, ((1, 64),)),
    }


def apply_ham(state, blocks_f32, partner_grid, row_mask):
    state_grid = state.reshape(BANDS, PLANES, 4, NB)

    def plane_apply(plane):
        below = jnp.take(state_grid, (plane + PLANES - 1) % PLANES, axis=1)
        middle = jnp.take(state_grid, plane, axis=1)
        above = jnp.take(state_grid, (plane + 1) % PLANES, axis=1)
        partner = jnp.take(partner_grid, plane, axis=0)
        columns = [middle]
        for slot_no in range(4):
            columns.append(middle[:, partner[:, slot_no]])
        columns.append(below[:, partner[:, 4]])
        columns.append(above[:, partner[:, 5]])
        sources = jnp.stack(columns, axis=2).reshape(BANDS, 4, 7 * NB).astype(jnp.float32)
        plane_blocks = jnp.take(blocks_f32, plane, axis=0)
        return jnp.einsum("bij,ijl->ibl", sources, plane_blocks, precision=lax.Precision.HIGHEST,
                          preferred_element_type=jnp.float32)

    stacked = lax.map(plane_apply, jnp.arange(PLANES, dtype=jnp.int32))
    return stacked.transpose(2, 0, 1, 3).reshape(BANDS, ROWS) * row_mask


def reference(start_bands, hamiltonian, neighbours, basis_count, owner_rows, rotation):
    basis_ids = lax.broadcasted_iota(jnp.int32, (ELEMS, NB), 1)
    row_mask = (basis_ids < basis_count[:, None]).astype(jnp.float32).reshape(ROWS)
    blocks_f32 = hamiltonian.reshape(PLANES, 4, 7 * NB, NB).astype(jnp.float32)
    partner_grid = neighbours.reshape(PLANES, 4, 6)
    earlier = (start_bands.astype(jnp.float32) * row_mask).astype(jnp.bfloat16)
    current = (0.5 * apply_ham(earlier, blocks_f32, partner_grid, row_mask)).astype(jnp.bfloat16)
    for repeat in range(DEGREE - 1):
        following = (apply_ham(current, blocks_f32, partner_grid, row_mask) - earlier.astype(jnp.float32)).astype(jnp.bfloat16)
        earlier = current
        current = following
    filtered = current
    turned = jnp.dot(filtered.T, rotation, preferred_element_type=jnp.float32).astype(jnp.bfloat16)
    row_start = (jnp.cumsum(owner_rows) - owner_rows).astype(jnp.int32)
    slot_ids = jnp.arange(CAP, dtype=jnp.int32)
    group_ids = jnp.arange(GROUPS, dtype=jnp.int32)
    row_index = group_ids[:, None, None] * ROWS_GRP + row_start[None, :, None] + slot_ids[None, None, :]
    slot_keep = jnp.broadcast_to((slot_ids[None, :] < owner_rows[:, None])[None], row_index.shape).reshape(-1)
    picked = jnp.take(turned, jnp.minimum(row_index, ROWS - 1).reshape(-1).astype(jnp.int32), axis=0)
    rotated = jnp.where(slot_keep[:, None], picked, jnp.zeros((), jnp.bfloat16))
    return filtered, rotated
```

```python
import jax
import jax.numpy as jnp
from jax import lax
from jax.experimental import pallas as pl
from jax.experimental.pallas import tpu as pltpu
from jax.sharding import Mesh
from jax.sharding import PartitionSpec as P

DEGREE = 8
NB = 192
ELEMS_DEV = 4
ROWS = ELEMS_DEV * NB
BANDS_DEV = 32
CAP = 36
CAP_PAD = 40
Z = 16
QUAD = 4
BF16 = jnp.bfloat16
F32 = jnp.float32
BAND_AXES = ("z", "yl", "c")

VMEM = pl.BlockSpec(memory_space=pltpu.VMEM)
SMEM = pl.BlockSpec(memory_space=pltpu.SMEM)


def params(mib):
    return pltpu.CompilerParams(vmem_limit_bytes=mib << 20)


def lanes(i):
    return slice(NB * i, NB * (i + 1))


def column_mask(count, rows):
    return lax.broadcasted_iota(jnp.int32, (rows, NB), 1) < count


def mask_kernel(counts, start_ref, y_ref):
    for i in range(ELEMS_DEV):
        block = start_ref[:, lanes(i)]
        y_ref[:, lanes(i)] = jnp.where(
            column_mask(counts[i], BANDS_DEV), block, jnp.zeros_like(block)
        )


def couple_kernel(neighbours, counts, parity, h_ref, even_ref, odd_ref):
    even_ref[...] = jnp.zeros_like(even_ref)
    odd_ref[...] = jnp.zeros_like(odd_ref)
    slot_even = 6 - parity[0]
    slot_odd = 5 + parity[0]
    for i in range(ELEMS_DEV):
        keep = column_mask(counts[i], NB)
        for slot, out_ref in ((slot_even, even_ref), (slot_odd, odd_ref)):
            block = h_ref[i, slot]
            block = jnp.where(keep, block, jnp.zeros_like(block))
            source = neighbours[i, slot - 1]
            out_ref[pl.ds(pl.multiple_of(source * NB, NB), NB), lanes(i)] = block


def local_kernel(scale, has_prev, neighbours, counts, y_ref, *refs):
    if has_prev:
        prev_ref, h_ref, p_ref, split = refs
    else:
        h_ref, p_ref, split = refs
    for i in range(ELEMS_DEV):
        split[i] = y_ref[:, lanes(i)]
    for i in range(ELEMS_DEV):
        total = jnp.dot(split[i], h_ref[i, 0], preferred_element_type=F32)
        for slot in range(4):
            total += jnp.dot(
                split[neighbours[i, slot]], h_ref[i, slot + 1], preferred_element_type=F32
            )
        total = jnp.where(column_mask(counts[i], BANDS_DEV), total * scale, 0.0)
        if has_prev:
            total = total - prev_ref[:, lanes(i)].astype(F32)
        p_ref[:, lanes(i)] = total


def halo_kernel(scale, p_ref, even_ref, odd_ref, w_even_ref, w_odd_ref, y_ref):
    total = jnp.dot(even_ref[...], w_even_ref[...], preferred_element_type=F32)
    total += jnp.dot(odd_ref[...], w_odd_ref[...], preferred_element_type=F32)
    y_ref[...] = (p_ref[...] + total * scale).astype(BF16)


def pick_kernel(starts, counts, y_ref, out_ref, turned):
    for block in range(ROWS // 128):
        part = y_ref[:, 128 * block : 128 * (block + 1)].astype(F32)
        turned[128 * block : 128 * (block + 1), :] = part.T
    slot = lax.broadcasted_iota(jnp.int32, (CAP_PAD, QUAD * BANDS_DEV), 0)
    for z in range(Z):
        rows = turned[pl.ds(starts[z], CAP_PAD), :]
        out_ref[z] = jnp.where(slot < counts[z], rows, 0.0).astype(BF16)


def rotate_kernel(x_ref, r_ref, out_ref, gathered):
    @pl.when(pl.program_id(0) == 0)
    def _():
        for z in range(Z):
            gathered[:, 128 * z : 128 * (z + 1)] = x_ref[z]

    pieces = []
    for block in range(r_ref.shape[0] // 128):
        for piece in (0, 2, 1, 3):
            first = 128 * block + 32 * piece
            pieces.append(r_ref[first : first + 32, :])
    weights = jnp.concatenate(pieces, axis=0)
    product = lax.dot_general(
        gathered[...], weights, (((1,), (1,)), ((), ())), preferred_element_type=F32
    )
    out_ref[...] = product[:CAP].astype(BF16)


def per_device(start_bands, hamiltonian, neighbours, basis_count, owner_rows, rotation):
    elem_size = lax.axis_size("elem")
    near = [(i, i ^ 1) for i in range(elem_size)]
    far = [(i, (i + 1 if i % 2 else i - 1) % elem_size) for i in range(elem_size)]
    parity = (lax.axis_index("elem") % 2).astype(jnp.int32).reshape(1)
    quad = lax.axis_index("yl") * 2 + lax.axis_index("c")
    row_starts = jnp.cumsum(owner_rows) - owner_rows
    my_starts = lax.dynamic_index_in_dim(row_starts.reshape(Z, QUAD), quad, 1, keepdims=False)
    my_counts = lax.dynamic_index_in_dim(owner_rows.reshape(Z, QUAD), quad, 1, keepdims=False)

    pieces = lax.all_gather(rotation.T, "yl", axis=0, tiled=True)
    rotation_all = lax.all_gather(pieces, ("z", "c"), axis=0, tiled=True)

    block_bf16 = jax.ShapeDtypeStruct((BANDS_DEV, ROWS), BF16)
    block_f32 = jax.ShapeDtypeStruct((BANDS_DEV, ROWS), F32)
    operator = jax.ShapeDtypeStruct((ROWS, ROWS), BF16)
    current = pl.pallas_call(
        mask_kernel, out_shape=block_bf16, in_specs=[SMEM, VMEM], out_specs=VMEM, compiler_params=params(4)
    )(basis_count, start_bands)
    w_even, w_odd = pl.pallas_call(
        couple_kernel,
        out_shape=(operator, operator),
        in_specs=[SMEM, SMEM, SMEM, VMEM],
        out_specs=(VMEM, VMEM),
        compiler_params=params(16),
    )(neighbours, basis_count, parity, hamiltonian)
    earlier = None
    for step in range(DEGREE):
        scale = 0.5 if step == 0 else 1.0
        from_far = lax.ppermute(current, "elem", far)
        from_near = lax.ppermute(current, "elem", near)
        previous = [] if earlier is None else [earlier]
        partial = pl.pallas_call(
            lambda *refs, scale=scale, has_prev=bool(previous): local_kernel(scale, has_prev, *refs),
            out_shape=block_f32,
            in_specs=[SMEM, SMEM, VMEM] + [VMEM] * len(previous) + [VMEM],
            out_specs=VMEM,
            scratch_shapes=[pltpu.VMEM((ELEMS_DEV, BANDS_DEV, NB), BF16)],
            compiler_params=params(8),
            cost_estimate=pl.CostEstimate(flops=3 * 10**8, bytes_accessed=3 << 20, transcendentals=0),
            name="local",
        )(neighbours, basis_count, current, *previous, hamiltonian)
        following = pl.pallas_call(
            lambda *refs, scale=scale: halo_kernel(scale, *refs),
            out_shape=block_bf16,
            in_specs=[VMEM] * 5,
            out_specs=VMEM,
            compiler_params=params(8),
            name="halo",
        )(partial, from_near, from_far, w_even, w_odd)
        earlier, current = current, following

    bands_quad = lax.all_gather(current, ("yl", "c"), axis=0, tiled=True)
    sent = pl.pallas_call(
        pick_kernel,
        out_shape=jax.ShapeDtypeStruct((Z, CAP_PAD, QUAD * BANDS_DEV), BF16),
        in_specs=[SMEM, SMEM, VMEM],
        out_specs=VMEM,
        scratch_shapes=[pltpu.VMEM((ROWS + 48, QUAD * BANDS_DEV), F32)],
        compiler_params=params(8),
        name="pick",
    )(my_starts, my_counts, bands_quad)
    received = lax.all_to_all(sent, "z", split_axis=0, concat_axis=0, tiled=True)
    bands = rotation_all.shape[1]
    tile = 256
    rotated = pl.pallas_call(
        rotate_kernel,
        out_shape=jax.ShapeDtypeStruct((CAP, bands), BF16),
        grid=(bands // tile,),
        in_specs=[
            pl.BlockSpec((Z, CAP_PAD, QUAD * BANDS_DEV), lambda n: (0, 0, 0)),
            pl.BlockSpec((tile, bands), lambda n: (n, 0)),
        ],
        out_specs=pl.BlockSpec((CAP, tile), lambda n: (0, n)),
        scratch_shapes=[pltpu.VMEM((CAP_PAD, bands), BF16)],
        compiler_params=params(16),
        name="rotate",
    )(received, rotation_all)
    return current, rotated


def solution(mesh):
    fine = Mesh(mesh.devices.reshape(mesh.shape["elem"], Z, 2, 2), ("elem",) + BAND_AXES)
    placed = (
        P(BAND_AXES, "elem"),
        P("elem", None, None, None),
        P("elem", None),
        P("elem"),
        P(),
        P(None, BAND_AXES),
    )
    return jax.shard_map(
        per_device,
        mesh=fine,
        in_specs=placed,
        out_specs=(P(BAND_AXES, "elem"), P(("elem",) + BAND_AXES, None)),
        check_vma=False,
    )
```

```python
import jax
import jax.numpy as jnp
from jax import lax
from jax.experimental import pallas as pl
from jax.experimental.pallas import tpu as pltpu
from jax.sharding import Mesh
from jax.sharding import PartitionSpec as P


DEGREE = 8
NB = 192
ELEMS_DEV = 4
ROWS = ELEMS_DEV * NB
BANDS_DEV = 32
CAP = 36
CAP_PAD = 40
Z = 16
QUAD = 4
BF16 = jnp.bfloat16
F32 = jnp.float32
TILE = 256
BAND_AXES = ("z", "yl", "c")

VMEM = pl.BlockSpec(memory_space=pltpu.VMEM)
SMEM = pl.BlockSpec(memory_space=pltpu.SMEM)


def params(mib):
    return pltpu.CompilerParams(vmem_limit_bytes=mib << 20)


def lanes(i):
    return slice(NB * i, NB * (i + 1))


def column_mask(count, rows):
    return lax.broadcasted_iota(jnp.int32, (rows, NB), 1) < count


def couple_kernel(neighbours, counts, parity, h_ref, even_ref, odd_ref):
    even_ref[...] = jnp.zeros_like(even_ref)
    odd_ref[...] = jnp.zeros_like(odd_ref)
    slot_even = 6 - parity[0]
    slot_odd = 5 + parity[0]
    for i in range(ELEMS_DEV):
        keep = column_mask(counts[i], NB)
        for slot, out_ref in ((slot_even, even_ref), (slot_odd, odd_ref)):
            block = h_ref[i, slot]
            block = jnp.where(keep, block, jnp.zeros_like(block))
            source = neighbours[i, slot - 1]
            out_ref[pl.ds(pl.multiple_of(source * NB, NB), NB), lanes(i)] = block


def local_kernel(scale, has_prev, neighbours, counts, y_ref, *refs):
    if has_prev:
        prev_ref, h_ref, p_ref, split = refs
    else:
        h_ref, p_ref, split = refs
    for i in range(ELEMS_DEV):
        split[i] = y_ref[:, lanes(i)]
    for i in range(ELEMS_DEV):
        total = jnp.dot(split[i], h_ref[i, 0], preferred_element_type=F32)
        for slot in range(4):
            total += jnp.dot(
                split[neighbours[i, slot]], h_ref[i, slot + 1], preferred_element_type=F32
            )
        total = jnp.where(column_mask(counts[i], BANDS_DEV), total * scale, 0.0)
        if has_prev:
            total = total - prev_ref[:, lanes(i)].astype(F32)
        p_ref[:, lanes(i)] = total


def halo_kernel(scale, p_ref, even_ref, odd_ref, w_even_ref, w_odd_ref, y_ref):
    total = jnp.dot(even_ref[...], w_even_ref[...], preferred_element_type=F32)
    total += jnp.dot(odd_ref[...], w_odd_ref[...], preferred_element_type=F32)
    y_ref[...] = (p_ref[...] + total * scale).astype(BF16)


def pick_kernel(starts, counts, y_ref, out_ref, turned):
    for block in range(ROWS // 128):
        part = y_ref[:, 128 * block : 128 * (block + 1)].astype(F32)
        turned[128 * block : 128 * (block + 1), :] = part.T
    slot = lax.broadcasted_iota(jnp.int32, (CAP_PAD, QUAD * BANDS_DEV), 0)
    for z in range(Z):
        rows = turned[pl.ds(starts[z], CAP_PAD), :]
        out_ref[z] = jnp.where(slot < counts[z], rows, 0.0).astype(BF16)


def rotate_kernel(low, x_ref, r_hbm, out_ref, gathered, weights, sems):
    chunks = r_hbm.shape[0] // TILE
    copies = [
        pltpu.make_async_copy(
            r_hbm.at[pl.ds(TILE * n, TILE)], weights.at[pl.ds(TILE * n, TILE)], sems.at[n]
        )
        for n in range(chunks)
    ]
    for copy in copies:
        copy.start()
    for z in range(Z):
        gathered[:, 128 * z : 128 * (z + 1)] = x_ref[z]
    mine = low[0]
    for n in range(chunks):
        copies[n].wait()
        pieces = []
        for block in range(TILE // 128):
            for y, core in ((0, 0), (0, 1), (1, 0), (1, 1)):
                first = n * TILE + 128 * block + 64 * core + 32 * (y ^ mine)
                pieces.append(weights[pl.ds(pl.multiple_of(first, 32), 32), :])
        product = lax.dot_general(
            gathered[...],
            jnp.concatenate(pieces, axis=0),
            (((1,), (1,)), ((), ())),
            preferred_element_type=F32,
        )
        out_ref[:, TILE * n : TILE * (n + 1)] = product[:CAP].astype(BF16)


def per_device(start_bands, hamiltonian, neighbours, basis_count, owner_rows, rotation):
    elem_size = lax.axis_size("elem")
    near = [(i, i ^ 1) for i in range(elem_size)]
    far = [(i, (i + 1 if i % 2 else i - 1) % elem_size) for i in range(elem_size)]
    parity = (lax.axis_index("elem") % 2).astype(jnp.int32).reshape(1)
    low = lax.axis_index("yl").astype(jnp.int32).reshape(1)
    quad = lax.axis_index("yl") * 2 + lax.axis_index("c")
    row_starts = jnp.cumsum(owner_rows) - owner_rows
    my_starts = lax.dynamic_index_in_dim(row_starts.reshape(Z, QUAD), quad, 1, keepdims=False)
    my_counts = lax.dynamic_index_in_dim(owner_rows.reshape(Z, QUAD), quad, 1, keepdims=False)

    columns = rotation.T
    other_columns = lax.ppermute(columns, "yl", [(0, 1), (1, 0)])

    block_bf16 = jax.ShapeDtypeStruct((BANDS_DEV, ROWS), BF16)
    block_f32 = jax.ShapeDtypeStruct((BANDS_DEV, ROWS), F32)
    operator = jax.ShapeDtypeStruct((ROWS, ROWS), BF16)
    column = lax.broadcasted_iota(jnp.int32, (BANDS_DEV, ROWS), 1)
    keep = jnp.zeros((BANDS_DEV, ROWS), jnp.bool_)
    for i in range(ELEMS_DEV):
        keep = keep | ((column >= NB * i) & (column < NB * i + basis_count[i]))
    current = jnp.where(keep, start_bands, jnp.zeros_like(start_bands))
    w_even, w_odd = pl.pallas_call(
        couple_kernel,
        out_shape=(operator, operator),
        in_specs=[SMEM, SMEM, SMEM, VMEM],
        out_specs=(VMEM, VMEM),
        compiler_params=params(16),
    )(neighbours, basis_count, parity, hamiltonian)
    earlier = None
    for step in range(DEGREE):
        scale = 0.5 if step == 0 else 1.0
        from_near = lax.ppermute(current, "elem", near)
        from_far = lax.ppermute(current, "elem", far)
        previous = [] if earlier is None else [earlier]
        partial = pl.pallas_call(
            lambda *refs, scale=scale, has_prev=bool(previous): local_kernel(scale, has_prev, *refs),
            out_shape=block_f32,
            in_specs=[SMEM, SMEM, VMEM] + [VMEM] * len(previous) + [VMEM],
            out_specs=VMEM,
            scratch_shapes=[pltpu.VMEM((ELEMS_DEV, BANDS_DEV, NB), BF16)],
            compiler_params=params(8),
            cost_estimate=pl.CostEstimate(flops=3 * 10**8, bytes_accessed=3 << 20, transcendentals=0),
            name="local",
        )(neighbours, basis_count, current, *previous, hamiltonian)
        if step == 0:
            other_columns, partial = lax.optimization_barrier((other_columns, partial))
            pieces = jnp.concatenate([columns, other_columns], axis=0)
            rotation_all = lax.all_gather(pieces, ("z", "c"), axis=0, tiled=True)
        following = pl.pallas_call(
            lambda *refs, scale=scale: halo_kernel(scale, *refs),
            out_shape=block_bf16,
            in_specs=[VMEM] * 5,
            out_specs=VMEM,
            compiler_params=params(8),
            name="halo",
        )(partial, from_near, from_far, w_even, w_odd)
        earlier, current = current, following

    bands_quad = lax.all_gather(current, ("yl", "c"), axis=0, tiled=True)
    sent = pl.pallas_call(
        pick_kernel,
        out_shape=jax.ShapeDtypeStruct((Z, CAP_PAD, QUAD * BANDS_DEV), BF16),
        in_specs=[SMEM, SMEM, VMEM],
        out_specs=VMEM,
        scratch_shapes=[pltpu.VMEM((ROWS + 48, QUAD * BANDS_DEV), F32)],
        compiler_params=params(8),
        name="pick",
    )(my_starts, my_counts, bands_quad)
    sent, rotation_all = lax.optimization_barrier((sent, rotation_all))
    received = lax.all_to_all(sent, "z", split_axis=0, concat_axis=0, tiled=True)
    rotated = pl.pallas_call(
        rotate_kernel,
        out_shape=jax.ShapeDtypeStruct((CAP, rotation_all.shape[1]), BF16),
        in_specs=[SMEM, VMEM, pl.BlockSpec(memory_space=pltpu.HBM)],
        out_specs=VMEM,
        scratch_shapes=[
            pltpu.VMEM((CAP_PAD, rotation_all.shape[1]), BF16),
            pltpu.VMEM(rotation_all.shape, BF16),
            pltpu.SemaphoreType.DMA((rotation_all.shape[0] // TILE,)),
        ],
        compiler_params=params(58),
        name="rotate",
    )(low, received, rotation_all)
    return current, rotated


def solution(mesh):
    fine = Mesh(mesh.devices.reshape(mesh.shape["elem"], Z, 2, 2), ("elem",) + BAND_AXES)
    placed = (
        P(BAND_AXES, "elem"),
        P("elem", None, None, None),
        P("elem", None),
        P("elem"),
        P(),
        P(None, BAND_AXES),
    )
    return jax.shard_map(
        per_device,
        mesh=fine,
        in_specs=placed,
        out_specs=(P(BAND_AXES, "elem"), P(("elem",) + BAND_AXES, None)),
        check_vma=False,
    )
```

```python
import jax
import jax.numpy as jnp
from jax import lax
from jax.experimental import pallas as pl
from jax.experimental.pallas import tpu as pltpu
from jax.sharding import Mesh
from jax.sharding import PartitionSpec as P


DEGREE = 8
NB = 192
ELEMS_DEV = 4
ROWS = ELEMS_DEV * NB
BANDS_DEV = 32
CAP = 36
CAP_PAD = 40
Z = 16
QUAD = 4
BF16 = jnp.bfloat16
F32 = jnp.float32
TILE = 256
BAND_AXES = ("z", "yl", "c")

VMEM = pl.BlockSpec(memory_space=pltpu.VMEM)
SMEM = pl.BlockSpec(memory_space=pltpu.SMEM)


def params(mib):
    return pltpu.CompilerParams(vmem_limit_bytes=mib << 20)


def lanes(i):
    return slice(NB * i, NB * (i + 1))


def column_mask(count, rows):
    return lax.broadcasted_iota(jnp.int32, (rows, NB), 1) < count


def mask_kernel(counts, start_ref, y_ref):
    for i in range(ELEMS_DEV):
        block = start_ref[:, lanes(i)]
        y_ref[:, lanes(i)] = jnp.where(
            column_mask(counts[i], BANDS_DEV), block, jnp.zeros_like(block)
        )


def couple_kernel(neighbours, counts, parity, h_ref, even_ref, odd_ref):
    even_ref[...] = jnp.zeros_like(even_ref)
    odd_ref[...] = jnp.zeros_like(odd_ref)
    slot_even = 6 - parity[0]
    slot_odd = 5 + parity[0]
    for i in range(ELEMS_DEV):
        keep = column_mask(counts[i], NB)
        for slot, out_ref in ((slot_even, even_ref), (slot_odd, odd_ref)):
            block = h_ref[i, slot]
            block = jnp.where(keep, block, jnp.zeros_like(block))
            source = neighbours[i, slot - 1]
            out_ref[pl.ds(pl.multiple_of(source * NB, NB), NB), lanes(i)] = block


def inside_kernel(scale, has_prev, neighbours, counts, parity, y_ref, pair_ref, *refs):
    if has_prev:
        prev_ref, h_ref, w_ref, p_ref, split = refs
    else:
        h_ref, w_ref, p_ref, split = refs
    other = pl.multiple_of(BANDS_DEV * (1 - parity[0]), BANDS_DEV)
    near = jnp.dot(pair_ref[pl.ds(other, BANDS_DEV), :], w_ref[...], preferred_element_type=F32)
    for i in range(ELEMS_DEV):
        split[i] = y_ref[:, lanes(i)]
    for i in range(ELEMS_DEV):
        total = jnp.dot(split[i], h_ref[i, 0], preferred_element_type=F32)
        for slot in range(4):
            total += jnp.dot(
                split[neighbours[i, slot]], h_ref[i, slot + 1], preferred_element_type=F32
            )
        total = jnp.where(column_mask(counts[i], BANDS_DEV), total, 0.0)
        total = (total + near[:, lanes(i)]) * scale
        if has_prev:
            total = total - prev_ref[:, lanes(i)].astype(F32)
        p_ref[:, lanes(i)] = total


def far_kernel(scale, p_ref, far_ref, w_ref, y_ref):
    total = jnp.dot(far_ref[...], w_ref[...], preferred_element_type=F32)
    y_ref[...] = (p_ref[...] + total * scale).astype(BF16)


def pick_kernel(starts, counts, y_ref, out_ref, turned):
    for block in range(ROWS // 128):
        part = y_ref[:, 128 * block : 128 * (block + 1)].astype(F32)
        turned[128 * block : 128 * (block + 1), :] = part.T
    slot = lax.broadcasted_iota(jnp.int32, (CAP_PAD, QUAD * BANDS_DEV), 0)
    for z in range(Z):
        rows = turned[pl.ds(starts[z], CAP_PAD), :]
        out_ref[z] = jnp.where(slot < counts[z], rows, 0.0).astype(BF16)


def rotate_kernel(low, x_ref, r_ref, out_ref, gathered):
    for z in range(Z):
        gathered[:, 128 * z : 128 * (z + 1)] = x_ref[z]
    mine = low[0]
    for n in range(r_ref.shape[0] // TILE):
        pieces = []
        for block in range(TILE // 128):
            for y, core in ((0, 0), (0, 1), (1, 0), (1, 1)):
                first = n * TILE + 128 * block + 64 * core + 32 * (y ^ mine)
                pieces.append(r_ref[pl.ds(pl.multiple_of(first, 32), 32), :])
        product = lax.dot_general(
            jnp.concatenate(pieces, axis=0),
            gathered[...],
            (((1,), (1,)), ((), ())),
            preferred_element_type=F32,
        )
        out_ref[:, TILE * n : TILE * (n + 1)] = product.T[:CAP].astype(BF16)


def per_device(start_bands, hamiltonian, neighbours, basis_count, owner_rows, rotation):
    elem_size = lax.axis_size("elem")
    near = [[i, i + 1] for i in range(0, elem_size, 2)]
    far = [(i, (i + 1 if i % 2 else i - 1) % elem_size) for i in range(elem_size)]
    parity = (lax.axis_index("elem") % 2).astype(jnp.int32).reshape(1)
    low = lax.axis_index("yl").astype(jnp.int32).reshape(1)
    quad = lax.axis_index("yl") * 2 + lax.axis_index("c")
    row_starts = jnp.cumsum(owner_rows) - owner_rows
    my_starts = lax.dynamic_index_in_dim(row_starts.reshape(Z, QUAD), quad, 1, keepdims=False)
    my_counts = lax.dynamic_index_in_dim(owner_rows.reshape(Z, QUAD), quad, 1, keepdims=False)

    columns = rotation.T

    block_bf16 = jax.ShapeDtypeStruct((BANDS_DEV, ROWS), BF16)
    block_f32 = jax.ShapeDtypeStruct((BANDS_DEV, ROWS), F32)
    operator = jax.ShapeDtypeStruct((ROWS, ROWS), BF16)
    current = pl.pallas_call(
        mask_kernel,
        out_shape=block_bf16,
        in_specs=[SMEM, VMEM],
        out_specs=VMEM,
        compiler_params=params(4),
        name="mask",
    )(basis_count, start_bands)
    w_even, w_odd = pl.pallas_call(
        couple_kernel,
        out_shape=(operator, operator),
        in_specs=[SMEM, SMEM, SMEM, VMEM],
        out_specs=(VMEM, VMEM),
        compiler_params=params(16),
    )(neighbours, basis_count, parity, hamiltonian)
    earlier = None
    for step in range(DEGREE):
        scale = 0.5 if step == 0 else 1.0
        previous = [] if earlier is None else [earlier]
        from_far = lax.ppermute(current, "elem", far)
        pair = lax.all_gather(
            current, "elem", axis=0, tiled=True, axis_index_groups=near
        )
        partial = pl.pallas_call(
            lambda *refs, scale=scale, has_prev=bool(previous): inside_kernel(
                scale, has_prev, *refs
            ),
            out_shape=block_f32,
            in_specs=[SMEM, SMEM, SMEM, VMEM, VMEM] + [VMEM] * len(previous) + [VMEM, VMEM],
            out_specs=VMEM,
            scratch_shapes=[pltpu.VMEM((ELEMS_DEV, BANDS_DEV, NB), BF16)],
            compiler_params=params(8),
            name="inside",
        )(neighbours, basis_count, parity, current, pair, *previous, hamiltonian, w_even)
        if step == 0:
            other_columns = lax.ppermute(columns, "yl", [(0, 1), (1, 0)])
            other_columns, partial = lax.optimization_barrier((other_columns, partial))
            pieces = jnp.concatenate([columns, other_columns], axis=0)
            rotation_all = lax.all_gather(pieces, ("z", "c"), axis=0, tiled=True)
        following = pl.pallas_call(
            lambda *refs, scale=scale: far_kernel(scale, *refs),
            out_shape=block_bf16,
            in_specs=[VMEM] * 3,
            out_specs=VMEM,
            compiler_params=params(8),
            name="outside",
        )(partial, from_far, w_odd)
        earlier, current = current, following

    filtered, rotation_all = lax.optimization_barrier((current, rotation_all))
    bands_quad = lax.all_gather(filtered, ("yl", "c"), axis=0, tiled=True)
    sent = pl.pallas_call(
        pick_kernel,
        out_shape=jax.ShapeDtypeStruct((Z, CAP_PAD, QUAD * BANDS_DEV), BF16),
        in_specs=[SMEM, SMEM, VMEM],
        out_specs=VMEM,
        scratch_shapes=[pltpu.VMEM((ROWS + 48, QUAD * BANDS_DEV), F32)],
        compiler_params=params(4),
        name="pick",
    )(my_starts, my_counts, bands_quad)
    received = lax.all_to_all(sent, "z", split_axis=0, concat_axis=0, tiled=True)
    rotated = pl.pallas_call(
        rotate_kernel,
        out_shape=jax.ShapeDtypeStruct((CAP, rotation_all.shape[1]), BF16),
        in_specs=[SMEM, VMEM, VMEM],
        out_specs=VMEM,
        scratch_shapes=[pltpu.VMEM((CAP_PAD, rotation_all.shape[1]), BF16)],
        compiler_params=params(4),
        name="rotate",
    )(low, received, rotation_all)
    return current, rotated


def solution(mesh):
    fine = Mesh(mesh.devices.reshape(mesh.shape["elem"], Z, 2, 2), ("elem",) + BAND_AXES)
    placed = (
        P(BAND_AXES, "elem"),
        P("elem", None, None, None),
        P("elem", None),
        P("elem"),
        P(),
        P(None, BAND_AXES),
    )
    return jax.shard_map(
        per_device,
        mesh=fine,
        in_specs=placed,
        out_specs=(P(BAND_AXES, "elem"), P(("elem",) + BAND_AXES, None)),
        check_vma=False,
    )
```

```python
import jax
import jax.numpy as jnp
from jax import lax
from jax.experimental import pallas as pl
from jax.experimental.pallas import tpu as pltpu
from jax.sharding import Mesh
from jax.sharding import PartitionSpec as P


DEGREE = 8
NB = 192
ELEMS_DEV = 4
ROWS = ELEMS_DEV * NB
BANDS_DEV = 32
CAP = 36
CAP_PAD = 40
Z = 16
QUAD = 4
BF16 = jnp.bfloat16
F32 = jnp.float32
TILE = 256
BAND_AXES = ("z", "yl", "c")

COST = pl.CostEstimate(flops=1 << 20, bytes_accessed=16 << 20, transcendentals=0)
VMEM = pl.BlockSpec(memory_space=pltpu.VMEM)
SMEM = pl.BlockSpec(memory_space=pltpu.SMEM)


def params(mib):
    return pltpu.CompilerParams(vmem_limit_bytes=mib << 20)


def lanes(i):
    return slice(NB * i, NB * (i + 1))


def column_mask(count, rows):
    return lax.broadcasted_iota(jnp.int32, (rows, NB), 1) < count


def mask_kernel(counts, start_ref, y_ref):
    for i in range(ELEMS_DEV):
        block = start_ref[:, lanes(i)]
        y_ref[:, lanes(i)] = jnp.where(
            column_mask(counts[i], BANDS_DEV), block, jnp.zeros_like(block)
        )


def couple_kernel(neighbours, counts, parity, h_ref, inner_ref, outer_ref, column):
    inner_ref[ROWS:, :] = jnp.zeros((ROWS, ROWS), BF16)
    outer_ref[...] = jnp.zeros_like(outer_ref)
    slot_near = 6 - parity[0]
    slot_far = 5 + parity[0]
    for i in range(ELEMS_DEV):
        keep = column_mask(counts[i], NB)

        def block(slot, i=i, keep=keep):
            value = h_ref[i, slot]
            return jnp.where(keep, value, jnp.zeros_like(value))

        def rows(source):
            return pl.ds(pl.multiple_of(source * NB, NB), NB)

        column[...] = jnp.zeros_like(column)
        column[lanes(i), :] = block(0).astype(F32)
        for slot in range(1, 5):
            column[rows(neighbours[i, slot - 1]), :] += block(slot).astype(F32)
        inner_ref[:ROWS, lanes(i)] = column[...].astype(BF16)
        inner_ref[rows(ELEMS_DEV + neighbours[i, slot_near - 1]), lanes(i)] = block(slot_near)
        outer_ref[rows(neighbours[i, slot_far - 1]), lanes(i)] = block(slot_far)


def inside_kernel(scale, has_prev, y_ref, pair_ref, second_ref, *refs):
    if has_prev:
        prev_ref, w_ref, p_ref = refs
    else:
        w_ref, p_ref = refs
    near = jnp.where(
        second_ref[...] > 0.0, pair_ref[BANDS_DEV:, :].astype(F32), pair_ref[:BANDS_DEV, :].astype(F32)
    ).astype(BF16)
    total = jnp.dot(y_ref[...], w_ref[:ROWS, :], preferred_element_type=F32)
    total += jnp.dot(near, w_ref[ROWS:, :], preferred_element_type=F32)
    total = total * scale
    if has_prev:
        total = total - prev_ref[...].astype(F32)
    p_ref[...] = total


def outside_kernel(scale, p_ref, far_ref, w_ref, y_ref):
    total = jnp.dot(far_ref[...], w_ref[...], preferred_element_type=F32)
    y_ref[...] = (p_ref[...] + total * scale).astype(BF16)


def pick_kernel(starts, counts, y_ref, out_ref, turned):
    for block in range(ROWS // 128):
        part = y_ref[:, 128 * block : 128 * (block + 1)].astype(F32)
        turned[128 * block : 128 * (block + 1), :] = part.T
    slot = lax.broadcasted_iota(jnp.int32, (CAP_PAD, QUAD * BANDS_DEV), 0)
    for z in range(Z):
        rows = turned[pl.ds(starts[z], CAP_PAD), :]
        out_ref[z] = jnp.where(slot < counts[z], rows, 0.0).astype(BF16)


def rotate_kernel(low, x_ref, r_ref, out_ref, gathered):
    for z in range(Z):
        gathered[:, 128 * z : 128 * (z + 1)] = x_ref[z]
    mine = low[0]
    for n in range(r_ref.shape[0] // TILE):
        pieces = []
        for block in range(TILE // 128):
            for y, core in ((0, 0), (0, 1), (1, 0), (1, 1)):
                first = n * TILE + 128 * block + 64 * core + 32 * (y ^ mine)
                pieces.append(r_ref[pl.ds(pl.multiple_of(first, 32), 32), :])
        product = lax.dot_general(
            jnp.concatenate(pieces, axis=0),
            gathered[...],
            (((1,), (1,)), ((), ())),
            preferred_element_type=F32,
        )
        out_ref[:, TILE * n : TILE * (n + 1)] = product.T[:CAP].astype(BF16)


def per_device(start_bands, hamiltonian, neighbours, basis_count, owner_rows, rotation):
    elem_size = lax.axis_size("elem")
    near = [[i, i + 1] for i in range(0, elem_size, 2)]
    far = [(i, (i + 1 if i % 2 else i - 1) % elem_size) for i in range(elem_size)]
    parity = (lax.axis_index("elem") % 2).astype(jnp.int32).reshape(1)
    second = jnp.broadcast_to((1 - parity).astype(F32)[:, None], (1, ROWS))
    low = lax.axis_index("yl").astype(jnp.int32).reshape(1)
    quad = lax.axis_index("yl") * 2 + lax.axis_index("c")
    row_starts = jnp.cumsum(owner_rows) - owner_rows
    my_starts = lax.dynamic_index_in_dim(row_starts.reshape(Z, QUAD), quad, 1, keepdims=False)
    my_counts = lax.dynamic_index_in_dim(owner_rows.reshape(Z, QUAD), quad, 1, keepdims=False)

    columns = rotation.T

    block_bf16 = jax.ShapeDtypeStruct((BANDS_DEV, ROWS), BF16)
    block_f32 = jax.ShapeDtypeStruct((BANDS_DEV, ROWS), F32)
    current = pl.pallas_call(
        mask_kernel,
        out_shape=block_bf16,
        in_specs=[SMEM, VMEM],
        out_specs=VMEM,
        compiler_params=params(4),
        name="mask",
    )(basis_count, start_bands)
    w_inner, w_outer = pl.pallas_call(
        couple_kernel,
        out_shape=(
            jax.ShapeDtypeStruct((2 * ROWS, ROWS), BF16),
            jax.ShapeDtypeStruct((ROWS, ROWS), BF16),
        ),
        in_specs=[SMEM, SMEM, SMEM, VMEM],
        out_specs=(VMEM, VMEM),
        scratch_shapes=[pltpu.VMEM((ROWS, NB), F32)],
        compiler_params=params(12),
        name="couple",
    )(neighbours, basis_count, parity, hamiltonian)
    earlier = None
    for step in range(DEGREE):
        scale = 0.5 if step == 0 else 1.0
        previous = [] if earlier is None else [earlier]
        from_far = lax.ppermute(current, "elem", far)
        mine = current
        if step == 0:
            other_columns = lax.ppermute(columns, "yl", [(0, 1), (1, 0)])
            pieces = jnp.concatenate([columns, other_columns], axis=0)
            pieces, mine, w_inner = lax.optimization_barrier((pieces, mine, w_inner))
            rotation_all = lax.all_gather(pieces, ("z", "c"), axis=0, tiled=True)
        pair = lax.all_gather(mine, "elem", axis=0, tiled=True, axis_index_groups=near)
        partial = pl.pallas_call(
            lambda *refs, scale=scale, has_prev=bool(previous): inside_kernel(
                scale, has_prev, *refs
            ),
            out_shape=block_f32,
            in_specs=[VMEM] * (4 + len(previous)),
            out_specs=VMEM,
            compiler_params=params(4),
            cost_estimate=COST,
            name="inside",
        )(mine, pair, second, *previous, w_inner)
        following = pl.pallas_call(
            lambda *refs, scale=scale: outside_kernel(scale, *refs),
            out_shape=block_bf16,
            in_specs=[VMEM] * 3,
            out_specs=VMEM,
            compiler_params=params(4),
            cost_estimate=COST,
            name="outside",
        )(partial, from_far, w_outer)
        earlier, current = current, following

    bands_quad = lax.all_gather(current, ("yl", "c"), axis=0, tiled=True)
    bands_quad, rotation_all = lax.optimization_barrier((bands_quad, rotation_all))
    sent = pl.pallas_call(
        pick_kernel,
        out_shape=jax.ShapeDtypeStruct((Z, CAP_PAD, QUAD * BANDS_DEV), BF16),
        in_specs=[SMEM, SMEM, VMEM],
        out_specs=VMEM,
        scratch_shapes=[pltpu.VMEM((ROWS + 48, QUAD * BANDS_DEV), F32)],
        compiler_params=params(4),
        cost_estimate=COST,
        name="pick",
    )(my_starts, my_counts, bands_quad)
    received = lax.all_to_all(sent, "z", split_axis=0, concat_axis=0, tiled=True)
    rotated = pl.pallas_call(
        rotate_kernel,
        out_shape=jax.ShapeDtypeStruct((CAP, rotation_all.shape[1]), BF16),
        in_specs=[SMEM, VMEM, VMEM],
        out_specs=VMEM,
        scratch_shapes=[pltpu.VMEM((CAP_PAD, rotation_all.shape[1]), BF16)],
        compiler_params=params(4),
        name="rotate",
    )(low, received, rotation_all)
    return current, rotated


def solution(mesh):
    fine = Mesh(mesh.devices.reshape(mesh.shape["elem"], Z, 2, 2), ("elem",) + BAND_AXES)
    placed = (
        P(BAND_AXES, "elem"),
        P("elem", None, None, None),
        P("elem", None),
        P("elem"),
        P(),
        P(None, BAND_AXES),
    )
    return jax.shard_map(
        per_device,
        mesh=fine,
        in_specs=placed,
        out_specs=(P(BAND_AXES, "elem"), P(("elem",) + BAND_AXES, None)),
        check_vma=False,
    )
```

```python
import jax
import jax.numpy as jnp
from jax import lax
from jax.experimental import pallas as pl
from jax.experimental.pallas import tpu as pltpu
from jax.sharding import Mesh
from jax.sharding import PartitionSpec as P


DEGREE = 8
NB = 192
ELEMS_DEV = 4
ROWS = ELEMS_DEV * NB
BANDS_DEV = 32
CAP = 36
CAP_PAD = 40
Z = 16
QUAD = 4
BF16 = jnp.bfloat16
F32 = jnp.float32
TILE = 1024
BAND_AXES = ("z", "yl", "c")

COST = pl.CostEstimate(flops=3 * 10**8, bytes_accessed=3 << 20, transcendentals=0)
VMEM = pl.BlockSpec(memory_space=pltpu.VMEM)
SMEM = pl.BlockSpec(memory_space=pltpu.SMEM)


def params(mib):
    return pltpu.CompilerParams(vmem_limit_bytes=mib << 20)


def lanes(i):
    return slice(NB * i, NB * (i + 1))


def column_mask(count, rows):
    return lax.broadcasted_iota(jnp.int32, (rows, NB), 1) < count


def mask_kernel(counts, start_ref, y_ref):
    for i in range(ELEMS_DEV):
        block = start_ref[:, lanes(i)]
        y_ref[:, lanes(i)] = jnp.where(
            column_mask(counts[i], BANDS_DEV), block, jnp.zeros_like(block)
        )


def couple_kernel(neighbours, counts, parity, h_ref, inner_ref, outer_ref, column):
    inner_ref[ROWS:, :] = jnp.zeros((ROWS, ROWS), BF16)
    outer_ref[...] = jnp.zeros_like(outer_ref)
    slot_near = 6 - parity[0]
    slot_far = 5 + parity[0]
    for i in range(ELEMS_DEV):
        keep = column_mask(counts[i], NB)

        def block(slot, i=i, keep=keep):
            value = h_ref[i, slot]
            return jnp.where(keep, value, jnp.zeros_like(value))

        def rows(source):
            return pl.ds(pl.multiple_of(source * NB, NB), NB)

        column[...] = jnp.zeros_like(column)
        column[lanes(i), :] = block(0).astype(F32)
        for slot in range(1, 5):
            column[rows(neighbours[i, slot - 1]), :] += block(slot).astype(F32)
        inner_ref[:ROWS, lanes(i)] = column[...].astype(BF16)
        inner_ref[rows(ELEMS_DEV + neighbours[i, slot_near - 1]), lanes(i)] = block(slot_near)
        outer_ref[rows(neighbours[i, slot_far - 1]), lanes(i)] = block(slot_far)


def inside_kernel(scale, has_prev, y_ref, pair_ref, second_ref, *refs):
    if has_prev:
        prev_ref, w_ref, p_ref = refs
    else:
        w_ref, p_ref = refs
    near = jnp.where(
        second_ref[...] > 0.0, pair_ref[BANDS_DEV:, :].astype(F32), pair_ref[:BANDS_DEV, :].astype(F32)
    ).astype(BF16)
    total = jnp.dot(y_ref[...], w_ref[:ROWS, :], preferred_element_type=F32)
    total += jnp.dot(near, w_ref[ROWS:, :], preferred_element_type=F32)
    total = total * scale
    if has_prev:
        total = total - prev_ref[...].astype(F32)
    p_ref[...] = total


def outside_kernel(scale, p_ref, far_ref, w_ref, y_ref):
    total = jnp.dot(far_ref[...], w_ref[...], preferred_element_type=F32)
    y_ref[...] = (p_ref[...] + total * scale).astype(BF16)


def pick_kernel(owner_rows, quad, y_ref, out_ref, turned):
    for block in range(ROWS // 128):
        part = y_ref[:, 128 * block : 128 * (block + 1)].astype(F32)
        turned[128 * block : 128 * (block + 1), :] = part.T
    slot = lax.broadcasted_iota(jnp.int32, (CAP_PAD, QUAD * BANDS_DEV), 0)
    first = jnp.int32(0)
    for z in range(Z):
        counts = [owner_rows[QUAD * z + q] for q in range(QUAD)]
        start, count = first, counts[0]
        for q in range(1, QUAD):
            first = first + counts[q - 1]
            start = jnp.where(quad[0] == q, first, start)
            count = jnp.where(quad[0] == q, counts[q], count)
        first = first + counts[QUAD - 1]
        rows = turned[pl.ds(start, CAP_PAD), :]
        out_ref[z] = jnp.where(slot < count, rows, 0.0).astype(BF16)


def join_kernel(low, own_ref, other_ref, out_ref):
    half = own_ref.shape[0]
    out_ref[pl.ds(pl.multiple_of(half * low[0], half), half), :] = own_ref[...]
    out_ref[pl.ds(pl.multiple_of(half * (1 - low[0]), half), half), :] = other_ref[...]


def rotate_kernel(x_ref, r_ref, out_ref, gathered):
    @pl.when(pl.program_id(0) == 0)
    def _():
        for z in range(Z):
            gathered[:, 128 * z : 128 * (z + 1)] = x_ref[z]

    pieces = []
    for block in range(TILE // 128):
        for piece in (0, 2, 1, 3):
            first = 128 * block + 32 * piece
            pieces.append(r_ref[first : first + 32, :])
    product = lax.dot_general(
        jnp.concatenate(pieces, axis=0),
        gathered[...],
        (((1,), (1,)), ((), ())),
        preferred_element_type=F32,
    )
    out_ref[...] = product.T[:CAP].astype(BF16)


def per_device(start_bands, hamiltonian, neighbours, basis_count, owner_rows, rotation):
    elem_size = lax.axis_size("elem")
    near = [[i, i + 1] for i in range(0, elem_size, 2)]
    far = [(i, (i + 1 if i % 2 else i - 1) % elem_size) for i in range(elem_size)]
    parity = (lax.axis_index("elem") % 2).astype(jnp.int32).reshape(1)
    second = jnp.broadcast_to((1 - parity).astype(F32)[:, None], (1, ROWS))
    low = lax.axis_index("yl").astype(jnp.int32).reshape(1)
    quad = (lax.axis_index("yl") * 2 + lax.axis_index("c")).astype(jnp.int32).reshape(1)

    columns = rotation.T

    block_bf16 = jax.ShapeDtypeStruct((BANDS_DEV, ROWS), BF16)
    block_f32 = jax.ShapeDtypeStruct((BANDS_DEV, ROWS), F32)
    current = pl.pallas_call(
        mask_kernel,
        out_shape=block_bf16,
        in_specs=[SMEM, VMEM],
        out_specs=VMEM,
        compiler_params=params(8),
        cost_estimate=COST,
        name="mask",
    )(basis_count, start_bands)
    earlier = None
    for step in range(DEGREE):
        scale = 0.5 if step == 0 else 1.0
        previous = [] if earlier is None else [earlier]
        from_far = lax.ppermute(current, "elem", far)
        pair = lax.all_gather(current, "elem", axis=0, tiled=True, axis_index_groups=near)
        if step == 0:
            other_columns = lax.ppermute(columns, "yl", [(0, 1), (1, 0)])
            other_columns, pair = lax.optimization_barrier((other_columns, pair))
            pieces = pl.pallas_call(
                join_kernel,
                out_shape=jax.ShapeDtypeStruct((2 * BANDS_DEV, columns.shape[1]), BF16),
                in_specs=[SMEM, VMEM, VMEM],
                out_specs=VMEM,
                compiler_params=params(8),
                cost_estimate=COST,
                name="join",
            )(low, columns, other_columns)
            pieces, parity, second, quad = lax.optimization_barrier((pieces, parity, second, quad))
            rotation_all = lax.all_gather(pieces, ("z", "c"), axis=0, tiled=True)
            w_inner, w_outer = pl.pallas_call(
                couple_kernel,
                out_shape=(
                    jax.ShapeDtypeStruct((2 * ROWS, ROWS), BF16),
                    jax.ShapeDtypeStruct((ROWS, ROWS), BF16),
                ),
                in_specs=[SMEM, SMEM, SMEM, VMEM],
                out_specs=(VMEM, VMEM),
                scratch_shapes=[pltpu.VMEM((ROWS, NB), F32)],
                compiler_params=params(12),
                name="couple",
            )(neighbours, basis_count, parity, hamiltonian)
        partial = pl.pallas_call(
            lambda *refs, scale=scale, has_prev=bool(previous): inside_kernel(
                scale, has_prev, *refs
            ),
            out_shape=block_f32,
            in_specs=[VMEM] * (4 + len(previous)),
            out_specs=VMEM,
            compiler_params=params(8),
            cost_estimate=COST,
            name="inside",
        )(current, pair, second, *previous, w_inner)
        following = pl.pallas_call(
            lambda *refs, scale=scale: outside_kernel(scale, *refs),
            out_shape=block_bf16,
            in_specs=[VMEM] * 3,
            out_specs=VMEM,
            compiler_params=params(8),
            cost_estimate=COST,
            name="outside",
        )(partial, from_far, w_outer)
        earlier, current = current, following

    bands_quad = lax.all_gather(current, ("yl", "c"), axis=0, tiled=True)
    sent = pl.pallas_call(
        pick_kernel,
        out_shape=jax.ShapeDtypeStruct((Z, CAP_PAD, QUAD * BANDS_DEV), BF16),
        in_specs=[SMEM, SMEM, VMEM],
        out_specs=VMEM,
        scratch_shapes=[pltpu.VMEM((ROWS + 48, QUAD * BANDS_DEV), F32)],
        compiler_params=params(8),
        cost_estimate=COST,
        name="pick",
    )(owner_rows, quad, bands_quad)
    received = lax.all_to_all(sent, "z", split_axis=0, concat_axis=0, tiled=True)
    rotated = pl.pallas_call(
        rotate_kernel,
        out_shape=jax.ShapeDtypeStruct((CAP, rotation_all.shape[1]), BF16),
        grid=(rotation_all.shape[0] // TILE,),
        in_specs=[
            pl.BlockSpec(received.shape, lambda n: (0, 0, 0)),
            pl.BlockSpec((TILE, rotation_all.shape[1]), lambda n: (n, 0)),
        ],
        out_specs=pl.BlockSpec((CAP, TILE), lambda n: (0, n)),
        scratch_shapes=[pltpu.VMEM((CAP_PAD, rotation_all.shape[1]), BF16)],
        compiler_params=params(58),
        name="rotate",
    )(received, rotation_all)
    return current, rotated


def solution(mesh):
    fine = Mesh(mesh.devices.reshape(mesh.shape["elem"], Z, 2, 2), ("elem",) + BAND_AXES)
    placed = (
        P(BAND_AXES, "elem"),
        P("elem", None, None, None),
        P("elem", None),
        P("elem"),
        P(),
        P(None, BAND_AXES),
    )
    return jax.shard_map(
        per_device,
        mesh=fine,
        in_specs=placed,
        out_specs=(P(BAND_AXES, "elem"), P(("elem",) + BAND_AXES, None)),
        check_vma=False,
    )
```

```python
import jax
import jax.numpy as jnp
from jax import lax
from jax.experimental import pallas as pl
from jax.experimental.pallas import tpu as pltpu
from jax.sharding import Mesh
from jax.sharding import PartitionSpec as P


DEGREE = 8
NB = 192
ELEMS_DEV = 4
ROWS = ELEMS_DEV * NB
BANDS_DEV = 32
CAP = 36
CAP_PAD = 40
Z = 16
QUAD = 4
BF16 = jnp.bfloat16
F32 = jnp.float32
TILE = 1024
BAND_AXES = ("z", "yl", "c")

COST = pl.CostEstimate(flops=3 * 10**8, bytes_accessed=3 << 20, transcendentals=0)
VMEM = pl.BlockSpec(memory_space=pltpu.VMEM)
SMEM = pl.BlockSpec(memory_space=pltpu.SMEM)


def params(mib):
    return pltpu.CompilerParams(vmem_limit_bytes=mib << 20)


def lanes(i):
    return slice(NB * i, NB * (i + 1))


def column_mask(count, rows):
    return lax.broadcasted_iota(jnp.int32, (rows, NB), 1) < count


def mask_kernel(counts, start_ref, y_ref):
    for i in range(ELEMS_DEV):
        block = start_ref[:, lanes(i)]
        y_ref[:, lanes(i)] = jnp.where(
            column_mask(counts[i], BANDS_DEV), block, jnp.zeros_like(block)
        )


def couple_kernel(neighbours, counts, parity, h_ref, inner_ref, outer_ref, column):
    inner_ref[ROWS:, :] = jnp.zeros((ROWS, ROWS), BF16)
    outer_ref[...] = jnp.zeros_like(outer_ref)
    slot_near = 6 - parity[0]
    slot_far = 5 + parity[0]
    for i in range(ELEMS_DEV):
        keep = column_mask(counts[i], NB)

        def block(slot, i=i, keep=keep):
            value = h_ref[i, slot]
            return jnp.where(keep, value, jnp.zeros_like(value))

        def rows(source):
            return pl.ds(pl.multiple_of(source * NB, NB), NB)

        column[...] = jnp.zeros_like(column)
        column[lanes(i), :] = block(0).astype(F32)
        for slot in range(1, 5):
            column[rows(neighbours[i, slot - 1]), :] += block(slot).astype(F32)
        inner_ref[:ROWS, lanes(i)] = column[...].astype(BF16)
        inner_ref[rows(ELEMS_DEV + neighbours[i, slot_near - 1]), lanes(i)] = block(slot_near)
        outer_ref[rows(neighbours[i, slot_far - 1]), lanes(i)] = block(slot_far)


def inside_kernel(scale, has_prev, y_ref, pair_ref, second_ref, *refs):
    if has_prev:
        prev_ref, w_ref, p_ref = refs
    else:
        w_ref, p_ref = refs
    near = jnp.where(
        second_ref[...] > 0.0, pair_ref[BANDS_DEV:, :].astype(F32), pair_ref[:BANDS_DEV, :].astype(F32)
    ).astype(BF16)
    total = jnp.dot(y_ref[...], w_ref[:ROWS, :], preferred_element_type=F32)
    total += jnp.dot(near, w_ref[ROWS:, :], preferred_element_type=F32)
    total = total * scale
    if has_prev:
        total = total - prev_ref[...].astype(F32)
    p_ref[...] = total


def outside_kernel(scale, p_ref, far_ref, w_ref, y_ref):
    total = jnp.dot(far_ref[...], w_ref[...], preferred_element_type=F32)
    y_ref[...] = (p_ref[...] + total * scale).astype(BF16)


def pick_kernel(owner_rows, quad, y_ref, out_ref, turned):
    for block in range(ROWS // 128):
        part = y_ref[:, 128 * block : 128 * (block + 1)].astype(F32)
        turned[128 * block : 128 * (block + 1), :] = part.T
    slot = lax.broadcasted_iota(jnp.int32, (CAP_PAD, QUAD * BANDS_DEV), 0)
    first = jnp.int32(0)
    for z in range(Z):
        counts = [owner_rows[QUAD * z + q] for q in range(QUAD)]
        start, count = first, counts[0]
        for q in range(1, QUAD):
            first = first + counts[q - 1]
            start = jnp.where(quad[0] == q, first, start)
            count = jnp.where(quad[0] == q, counts[q], count)
        first = first + counts[QUAD - 1]
        rows = turned[pl.ds(start, CAP_PAD), :]
        out_ref[z] = jnp.where(slot < count, rows, 0.0).astype(BF16)


def emit_kernel(y_ref, out_ref):
    out_ref[...] = y_ref[...]


def join_kernel(low, own_ref, other_ref, out_ref):
    half = own_ref.shape[0]
    out_ref[pl.ds(pl.multiple_of(half * low[0], half), half), :] = own_ref[...]
    out_ref[pl.ds(pl.multiple_of(half * (1 - low[0]), half), half), :] = other_ref[...]


def rotate_kernel(x_ref, r_ref, out_ref, gathered):
    @pl.when(pl.program_id(0) == 0)
    def _():
        for z in range(Z):
            gathered[:, 128 * z : 128 * (z + 1)] = x_ref[z]

    pieces = []
    for block in range(TILE // 128):
        for piece in (0, 2, 1, 3):
            first = 128 * block + 32 * piece
            pieces.append(r_ref[first : first + 32, :])
    product = lax.dot_general(
        jnp.concatenate(pieces, axis=0),
        gathered[...],
        (((1,), (1,)), ((), ())),
        preferred_element_type=F32,
    )
    out_ref[...] = product.T[:CAP].astype(BF16)


def per_device(start_bands, hamiltonian, neighbours, basis_count, owner_rows, rotation):
    elem_size = lax.axis_size("elem")
    near = [[i, i + 1] for i in range(0, elem_size, 2)]
    far = [(i, (i + 1 if i % 2 else i - 1) % elem_size) for i in range(elem_size)]
    parity = (lax.axis_index("elem") % 2).astype(jnp.int32).reshape(1)
    second = jnp.broadcast_to((1 - parity).astype(F32)[:, None], (1, ROWS))
    low = lax.axis_index("yl").astype(jnp.int32).reshape(1)
    quad = (lax.axis_index("yl") * 2 + lax.axis_index("c")).astype(jnp.int32).reshape(1)

    columns = rotation.T

    block_bf16 = jax.ShapeDtypeStruct((BANDS_DEV, ROWS), BF16)
    block_f32 = jax.ShapeDtypeStruct((BANDS_DEV, ROWS), F32)
    current = pl.pallas_call(
        mask_kernel,
        out_shape=block_bf16,
        in_specs=[SMEM, VMEM],
        out_specs=VMEM,
        compiler_params=params(8),
        cost_estimate=COST,
        name="mask",
    )(basis_count, start_bands)
    earlier = None
    for step in range(DEGREE):
        scale = 0.5 if step == 0 else 1.0
        previous = [] if earlier is None else [earlier]
        from_far = lax.ppermute(current, "elem", far)
        pair = lax.all_gather(current, "elem", axis=0, tiled=True, axis_index_groups=near)
        if step == 0:
            other_columns = lax.ppermute(columns, "yl", [(0, 1), (1, 0)])
            other_columns, pair = lax.optimization_barrier((other_columns, pair))
            pieces = pl.pallas_call(
                join_kernel,
                out_shape=jax.ShapeDtypeStruct((2 * BANDS_DEV, columns.shape[1]), BF16),
                in_specs=[SMEM, VMEM, VMEM],
                out_specs=VMEM,
                compiler_params=params(8),
                cost_estimate=COST,
                name="join",
            )(low, columns, other_columns)
            pieces, parity, second, quad = lax.optimization_barrier((pieces, parity, second, quad))
            rotation_all = lax.all_gather(pieces, ("z", "c"), axis=0, tiled=True)
            w_inner, w_outer = pl.pallas_call(
                couple_kernel,
                out_shape=(
                    jax.ShapeDtypeStruct((2 * ROWS, ROWS), BF16),
                    jax.ShapeDtypeStruct((ROWS, ROWS), BF16),
                ),
                in_specs=[SMEM, SMEM, SMEM, VMEM],
                out_specs=(VMEM, VMEM),
                scratch_shapes=[pltpu.VMEM((ROWS, NB), F32)],
                compiler_params=params(12),
                name="couple",
            )(neighbours, basis_count, parity, hamiltonian)
        partial = pl.pallas_call(
            lambda *refs, scale=scale, has_prev=bool(previous): inside_kernel(
                scale, has_prev, *refs
            ),
            out_shape=block_f32,
            in_specs=[VMEM] * (4 + len(previous)),
            out_specs=VMEM,
            compiler_params=params(8),
            cost_estimate=COST,
            name="inside",
        )(current, pair, second, *previous, w_inner)
        following = pl.pallas_call(
            lambda *refs, scale=scale: outside_kernel(scale, *refs),
            out_shape=block_bf16,
            in_specs=[VMEM] * 3,
            out_specs=VMEM,
            compiler_params=params(8),
            cost_estimate=COST,
            name="outside",
        )(partial, from_far, w_outer)
        earlier, current = current, following

    bands_quad = lax.all_gather(current, ("yl", "c"), axis=0, tiled=True)
    sent = pl.pallas_call(
        pick_kernel,
        out_shape=jax.ShapeDtypeStruct((Z, CAP_PAD, QUAD * BANDS_DEV), BF16),
        in_specs=[SMEM, SMEM, VMEM],
        out_specs=VMEM,
        scratch_shapes=[pltpu.VMEM((ROWS + 48, QUAD * BANDS_DEV), F32)],
        compiler_params=params(8),
        cost_estimate=COST,
        name="pick",
    )(owner_rows, quad, bands_quad)
    filtered = pl.pallas_call(
        emit_kernel,
        out_shape=block_bf16,
        in_specs=[VMEM],
        out_specs=VMEM,
        compiler_params=params(8),
        cost_estimate=COST,
        name="emit",
    )(current)
    received = lax.all_to_all(sent, "z", split_axis=0, concat_axis=0, tiled=True)
    rotated = pl.pallas_call(
        rotate_kernel,
        out_shape=jax.ShapeDtypeStruct((CAP, rotation_all.shape[1]), BF16),
        grid=(rotation_all.shape[0] // TILE,),
        in_specs=[
            pl.BlockSpec(received.shape, lambda n: (0, 0, 0)),
            pl.BlockSpec((TILE, rotation_all.shape[1]), lambda n: (n, 0)),
        ],
        out_specs=pl.BlockSpec((CAP, TILE), lambda n: (0, n)),
        scratch_shapes=[pltpu.VMEM((CAP_PAD, rotation_all.shape[1]), BF16)],
        compiler_params=params(58),
        name="rotate",
    )(received, rotation_all)
    return filtered, rotated


def solution(mesh):
    fine = Mesh(mesh.devices.reshape(mesh.shape["elem"], Z, 2, 2), ("elem",) + BAND_AXES)
    placed = (
        P(BAND_AXES, "elem"),
        P("elem", None, None, None),
        P("elem", None),
        P("elem"),
        P(),
        P(None, BAND_AXES),
    )
    return jax.shard_map(
        per_device,
        mesh=fine,
        in_specs=placed,
        out_specs=(P(BAND_AXES, "elem"), P(("elem",) + BAND_AXES, None)),
        check_vma=False,
    )
```

```python
import jax
import jax.numpy as jnp
from jax import lax
from jax.experimental import pallas as pl
from jax.experimental.pallas import tpu as pltpu
from jax.sharding import Mesh
from jax.sharding import PartitionSpec as P


DEGREE = 8
NB = 192
ELEMS_DEV = 4
ROWS = ELEMS_DEV * NB
BANDS_DEV = 32
CAP = 36
CAP_PAD = 40
Z = 16
QUAD = 4
BF16 = jnp.bfloat16
F32 = jnp.float32
TILE = 1024
BAND_AXES = ("z", "yl", "c")

COST = pl.CostEstimate(flops=3 * 10**8, bytes_accessed=3 << 20, transcendentals=0)
VMEM = pl.BlockSpec(memory_space=pltpu.VMEM)
SMEM = pl.BlockSpec(memory_space=pltpu.SMEM)
HBM = pl.BlockSpec(memory_space=pltpu.HBM)


def in_hbm(value):
    return pltpu.with_memory_space_constraint(value, pltpu.HBM)


def params(mib):
    return pltpu.CompilerParams(vmem_limit_bytes=mib << 20)


def lanes(i):
    return slice(NB * i, NB * (i + 1))


def column_mask(count, rows):
    return lax.broadcasted_iota(jnp.int32, (rows, NB), 1) < count


def mask_kernel(counts_hbm, start_hbm, y_ref, counts, start, sems):
    small = pltpu.make_async_copy(counts_hbm, counts, sems.at[0])
    large = pltpu.make_async_copy(start_hbm, start, sems.at[1])
    small.start()
    large.start()
    small.wait()
    large.wait()
    for i in range(ELEMS_DEV):
        block = start[:, lanes(i)]
        y_ref[:, lanes(i)] = jnp.where(
            column_mask(counts[i], BANDS_DEV), block, jnp.zeros_like(block)
        )


def couple_kernel(
    neighbours_hbm, counts_hbm, parity, h_hbm, inner_ref, outer_ref, column, h_ref, neighbours, counts, sems
):
    copies = [
        pltpu.make_async_copy(h_hbm.at[i], h_ref.at[i], sems.at[i]) for i in range(ELEMS_DEV)
    ]
    tables = [
        pltpu.make_async_copy(neighbours_hbm, neighbours, sems.at[ELEMS_DEV]),
        pltpu.make_async_copy(counts_hbm, counts, sems.at[ELEMS_DEV + 1]),
    ]
    for copy in tables + copies:
        copy.start()
    inner_ref[ROWS:, :] = jnp.zeros((ROWS, ROWS), BF16)
    outer_ref[...] = jnp.zeros_like(outer_ref)
    for copy in tables:
        copy.wait()
    slot_near = 6 - parity[0]
    slot_far = 5 + parity[0]
    for i in range(ELEMS_DEV):
        keep = column_mask(counts[i], NB)
        copies[i].wait()

        def block(slot, i=i, keep=keep):
            value = h_ref[i, slot]
            return jnp.where(keep, value, jnp.zeros_like(value))

        def rows(source):
            return pl.ds(pl.multiple_of(source * NB, NB), NB)

        column[...] = jnp.zeros_like(column)
        column[lanes(i), :] = block(0).astype(F32)
        for slot in range(1, 5):
            column[rows(neighbours[i, slot - 1]), :] += block(slot).astype(F32)
        inner_ref[:ROWS, lanes(i)] = column[...].astype(BF16)
        inner_ref[rows(ELEMS_DEV + neighbours[i, slot_near - 1]), lanes(i)] = block(slot_near)
        outer_ref[rows(neighbours[i, slot_far - 1]), lanes(i)] = block(slot_far)


def inside_kernel(scale, has_prev, y_ref, pair_ref, second_ref, *refs):
    if has_prev:
        prev_ref, w_ref, p_ref = refs
    else:
        w_ref, p_ref = refs
    near = jnp.where(
        second_ref[...] > 0.0, pair_ref[BANDS_DEV:, :].astype(F32), pair_ref[:BANDS_DEV, :].astype(F32)
    ).astype(BF16)
    total = jnp.dot(y_ref[...], w_ref[:ROWS, :], preferred_element_type=F32)
    total += jnp.dot(near, w_ref[ROWS:, :], preferred_element_type=F32)
    total = total * scale
    if has_prev:
        total = total - prev_ref[...].astype(F32)
    p_ref[...] = total


def outside_kernel(scale, p_ref, far_ref, w_ref, y_ref):
    total = jnp.dot(far_ref[...], w_ref[...], preferred_element_type=F32)
    y_ref[...] = (p_ref[...] + total * scale).astype(BF16)


def pick_kernel(owner_rows, quad, y_ref, out_ref, turned):
    for block in range(ROWS // 128):
        part = y_ref[:, 128 * block : 128 * (block + 1)].astype(F32)
        turned[128 * block : 128 * (block + 1), :] = part.T
    slot = lax.broadcasted_iota(jnp.int32, (CAP_PAD, QUAD * BANDS_DEV), 0)
    first = jnp.int32(0)
    for z in range(Z):
        counts = [owner_rows[QUAD * z + q] for q in range(QUAD)]
        start, count = first, counts[0]
        for q in range(1, QUAD):
            first = first + counts[q - 1]
            start = jnp.where(quad[0] == q, first, start)
            count = jnp.where(quad[0] == q, counts[q], count)
        first = first + counts[QUAD - 1]
        rows = turned[pl.ds(start, CAP_PAD), :]
        out_ref[z] = jnp.where(slot < count, rows, 0.0).astype(BF16)


def join_kernel(low, own_hbm, other_ref, out_ref, own, sem):
    copy = pltpu.make_async_copy(own_hbm, own, sem)
    copy.start()
    half = other_ref.shape[0]
    out_ref[pl.ds(pl.multiple_of(half * (1 - low[0]), half), half), :] = other_ref[...]
    copy.wait()
    out_ref[pl.ds(pl.multiple_of(half * low[0], half), half), :] = own[...]


def rotate_kernel(x_ref, r_ref, out_ref, gathered):
    @pl.when(pl.program_id(0) == 0)
    def _():
        for z in range(Z):
            gathered[:, 128 * z : 128 * (z + 1)] = x_ref[z]

    pieces = []
    for block in range(TILE // 128):
        for piece in (0, 2, 1, 3):
            first = 128 * block + 32 * piece
            pieces.append(r_ref[first : first + 32, :])
    product = lax.dot_general(
        jnp.concatenate(pieces, axis=0),
        gathered[...],
        (((1,), (1,)), ((), ())),
        preferred_element_type=F32,
    )
    out_ref[...] = product.T[:CAP].astype(BF16)


def per_device(start_bands, hamiltonian, neighbours, basis_count, owner_rows, rotation):
    elem_size = lax.axis_size("elem")
    near = [[i, i + 1] for i in range(0, elem_size, 2)]
    far = [(i, (i + 1 if i % 2 else i - 1) % elem_size) for i in range(elem_size)]
    parity = (lax.axis_index("elem") % 2).astype(jnp.int32).reshape(1)
    second = jnp.broadcast_to((1 - parity).astype(F32)[:, None], (1, ROWS))
    low = lax.axis_index("yl").astype(jnp.int32).reshape(1)
    quad = (lax.axis_index("yl") * 2 + lax.axis_index("c")).astype(jnp.int32).reshape(1)

    columns = rotation.T

    block_bf16 = jax.ShapeDtypeStruct((BANDS_DEV, ROWS), BF16)
    block_f32 = jax.ShapeDtypeStruct((BANDS_DEV, ROWS), F32)
    current = pl.pallas_call(
        mask_kernel,
        out_shape=block_bf16,
        in_specs=[HBM, HBM],
        out_specs=VMEM,
        scratch_shapes=[
            pltpu.SMEM(basis_count.shape, jnp.int32),
            pltpu.VMEM(start_bands.shape, BF16),
            pltpu.SemaphoreType.DMA((2,)),
        ],
        compiler_params=params(8),
        cost_estimate=COST,
        name="mask",
    )(in_hbm(basis_count), in_hbm(start_bands))
    earlier = None
    for step in range(DEGREE):
        scale = 0.5 if step == 0 else 1.0
        previous = [] if earlier is None else [earlier]
        from_far = lax.ppermute(current, "elem", far)
        pair = lax.all_gather(current, "elem", axis=0, tiled=True, axis_index_groups=near)
        if step == 0:
            other_columns = lax.ppermute(columns, "yl", [(0, 1), (1, 0)])
            other_columns, pair = lax.optimization_barrier((other_columns, pair))
            pieces = pl.pallas_call(
                join_kernel,
                out_shape=jax.ShapeDtypeStruct((2 * BANDS_DEV, columns.shape[1]), BF16),
                in_specs=[SMEM, HBM, VMEM],
                out_specs=VMEM,
                scratch_shapes=[pltpu.VMEM(columns.shape, BF16), pltpu.SemaphoreType.DMA],
                compiler_params=params(8),
                cost_estimate=COST,
                name="join",
            )(low, in_hbm(columns), other_columns)
            pieces, parity, second, quad = lax.optimization_barrier((pieces, parity, second, quad))
            rotation_all = lax.all_gather(pieces, ("z", "c"), axis=0, tiled=True)
            w_inner, w_outer = pl.pallas_call(
                couple_kernel,
                out_shape=(
                    jax.ShapeDtypeStruct((2 * ROWS, ROWS), BF16),
                    jax.ShapeDtypeStruct((ROWS, ROWS), BF16),
                ),
                in_specs=[HBM, HBM, SMEM, HBM],
                out_specs=(VMEM, VMEM),
                scratch_shapes=[
                pltpu.VMEM((ROWS, NB), F32),
                pltpu.VMEM(hamiltonian.shape, BF16),
                pltpu.SMEM(neighbours.shape, jnp.int32),
                pltpu.SMEM(basis_count.shape, jnp.int32),
                pltpu.SemaphoreType.DMA((ELEMS_DEV + 2,)),
            ],
                compiler_params=params(12),
                name="couple",
            )(in_hbm(neighbours), in_hbm(basis_count), parity, in_hbm(hamiltonian))
        partial = pl.pallas_call(
            lambda *refs, scale=scale, has_prev=bool(previous): inside_kernel(
                scale, has_prev, *refs
            ),
            out_shape=block_f32,
            in_specs=[VMEM] * (4 + len(previous)),
            out_specs=VMEM,
            compiler_params=params(8),
            cost_estimate=COST,
            name="inside",
        )(current, pair, second, *previous, w_inner)
        following = pl.pallas_call(
            lambda *refs, scale=scale: outside_kernel(scale, *refs),
            out_shape=block_bf16,
            in_specs=[VMEM] * 3,
            out_specs=VMEM,
            compiler_params=params(8),
            cost_estimate=COST,
            name="outside",
        )(partial, from_far, w_outer)
        earlier, current = current, following

    bands_quad = lax.all_gather(current, ("yl", "c"), axis=0, tiled=True)
    sent = pl.pallas_call(
        pick_kernel,
        out_shape=jax.ShapeDtypeStruct((Z, CAP_PAD, QUAD * BANDS_DEV), BF16),
        in_specs=[SMEM, SMEM, VMEM],
        out_specs=VMEM,
        scratch_shapes=[pltpu.VMEM((ROWS + 48, QUAD * BANDS_DEV), F32)],
        compiler_params=params(8),
        cost_estimate=COST,
        name="pick",
    )(owner_rows, quad, bands_quad)
    received = lax.all_to_all(sent, "z", split_axis=0, concat_axis=0, tiled=True)
    rotated = pl.pallas_call(
        rotate_kernel,
        out_shape=jax.ShapeDtypeStruct((CAP, rotation_all.shape[1]), BF16),
        grid=(rotation_all.shape[0] // TILE,),
        in_specs=[
            pl.BlockSpec(received.shape, lambda n: (0, 0, 0)),
            pl.BlockSpec((TILE, rotation_all.shape[1]), lambda n: (n, 0)),
        ],
        out_specs=pl.BlockSpec((CAP, TILE), lambda n: (0, n)),
        scratch_shapes=[pltpu.VMEM((CAP_PAD, rotation_all.shape[1]), BF16)],
        compiler_params=params(24),
        name="rotate",
    )(received, in_hbm(rotation_all))
    return current, rotated


def solution(mesh):
    fine = Mesh(mesh.devices.reshape(mesh.shape["elem"], Z, 2, 2), ("elem",) + BAND_AXES)
    placed = (
        P(BAND_AXES, "elem"),
        P("elem", None, None, None),
        P("elem", None),
        P("elem"),
        P(),
        P(None, BAND_AXES),
    )
    return jax.shard_map(
        per_device,
        mesh=fine,
        in_specs=placed,
        out_specs=(P(BAND_AXES, "elem"), P(("elem",) + BAND_AXES, None)),
        check_vma=False,
    )
```

```python
import jax
import jax.numpy as jnp
from jax import lax
from jax.experimental import pallas as pl
from jax.experimental.pallas import tpu as pltpu
from jax.sharding import Mesh
from jax.sharding import PartitionSpec as P


DEGREE = 8
NB = 192
ELEMS_DEV = 4
ROWS = ELEMS_DEV * NB
BANDS_DEV = 32
CAP = 36
CAP_PAD = 40
Z = 16
QUAD = 4
BF16 = jnp.bfloat16
F32 = jnp.float32
TILE = 1024
BAND_AXES = ("z", "yl", "c")

COST = pl.CostEstimate(flops=3 * 10**8, bytes_accessed=3 << 20, transcendentals=0)
VMEM = pl.BlockSpec(memory_space=pltpu.VMEM)
SMEM = pl.BlockSpec(memory_space=pltpu.SMEM)
HBM = pl.BlockSpec(memory_space=pltpu.HBM)


def in_hbm(value):
    return pltpu.with_memory_space_constraint(value, pltpu.HBM)


def params(mib):
    return pltpu.CompilerParams(vmem_limit_bytes=mib << 20)


def lanes(i):
    return slice(NB * i, NB * (i + 1))


def column_mask(count, rows):
    return lax.broadcasted_iota(jnp.int32, (rows, NB), 1) < count


def mask_kernel(counts_hbm, start_hbm, y_ref, counts, start, sems):
    small = pltpu.make_async_copy(counts_hbm, counts, sems.at[0])
    large = pltpu.make_async_copy(start_hbm, start, sems.at[1])
    small.start()
    large.start()
    small.wait()
    large.wait()
    for i in range(ELEMS_DEV):
        block = start[:, lanes(i)]
        y_ref[:, lanes(i)] = jnp.where(
            column_mask(counts[i], BANDS_DEV), block, jnp.zeros_like(block)
        )


def couple_kernel(
    neighbours_hbm, counts_hbm, parity, h_hbm, inner_ref, outer_ref, column, h_ref, neighbours, counts, sems
):
    copies = [
        pltpu.make_async_copy(h_hbm.at[i], h_ref.at[i], sems.at[i]) for i in range(ELEMS_DEV)
    ]
    tables = [
        pltpu.make_async_copy(neighbours_hbm, neighbours, sems.at[ELEMS_DEV]),
        pltpu.make_async_copy(counts_hbm, counts, sems.at[ELEMS_DEV + 1]),
    ]
    for copy in tables + copies:
        copy.start()
    inner_ref[ROWS:, :] = jnp.zeros((ROWS, ROWS), BF16)
    outer_ref[...] = jnp.zeros_like(outer_ref)
    for copy in tables:
        copy.wait()
    slot_near = 6 - parity[0]
    slot_far = 5 + parity[0]
    for i in range(ELEMS_DEV):
        keep = column_mask(counts[i], NB)
        copies[i].wait()

        def block(slot, i=i, keep=keep):
            value = h_ref[i, slot]
            return jnp.where(keep, value, jnp.zeros_like(value))

        def rows(source):
            return pl.ds(pl.multiple_of(source * NB, NB), NB)

        column[...] = jnp.zeros_like(column)
        column[lanes(i), :] = block(0).astype(F32)
        for slot in range(1, 5):
            column[rows(neighbours[i, slot - 1]), :] += block(slot).astype(F32)
        inner_ref[:ROWS, lanes(i)] = column[...].astype(BF16)
        inner_ref[rows(ELEMS_DEV + neighbours[i, slot_near - 1]), lanes(i)] = block(slot_near)
        outer_ref[rows(neighbours[i, slot_far - 1]), lanes(i)] = block(slot_far)


def inside_kernel(scale, has_prev, y_ref, pair_ref, second_ref, *refs):
    if has_prev:
        prev_ref, w_ref, p_ref = refs
    else:
        w_ref, p_ref = refs
    near = jnp.where(
        second_ref[...] > 0.0, pair_ref[BANDS_DEV:, :].astype(F32), pair_ref[:BANDS_DEV, :].astype(F32)
    ).astype(BF16)
    total = jnp.dot(y_ref[...], w_ref[:ROWS, :], preferred_element_type=F32)
    total += jnp.dot(near, w_ref[ROWS:, :], preferred_element_type=F32)
    total = total * scale
    if has_prev:
        total = total - prev_ref[...].astype(F32)
    p_ref[...] = total


def outside_kernel(scale, p_ref, far_ref, w_ref, y_ref):
    total = jnp.dot(far_ref[...], w_ref[...], preferred_element_type=F32)
    y_ref[...] = (p_ref[...] + total * scale).astype(BF16)


def pick_kernel(owner_rows, quad, y_ref, out_ref, own_ref, turned):
    own_ref[...] = y_ref[pl.ds(pl.multiple_of(BANDS_DEV * quad[0], BANDS_DEV), BANDS_DEV), :]
    for block in range(ROWS // 128):
        part = y_ref[:, 128 * block : 128 * (block + 1)].astype(F32)
        turned[128 * block : 128 * (block + 1), :] = part.T
    slot = lax.broadcasted_iota(jnp.int32, (CAP_PAD, QUAD * BANDS_DEV), 0)
    first = jnp.int32(0)
    for z in range(Z):
        counts = [owner_rows[QUAD * z + q] for q in range(QUAD)]
        start, count = first, counts[0]
        for q in range(1, QUAD):
            first = first + counts[q - 1]
            start = jnp.where(quad[0] == q, first, start)
            count = jnp.where(quad[0] == q, counts[q], count)
        first = first + counts[QUAD - 1]
        rows = turned[pl.ds(start, CAP_PAD), :]
        out_ref[z] = jnp.where(slot < count, rows, 0.0).astype(BF16)


def join_kernel(low, own_hbm, other_ref, out_hbm, own, sems):
    half = other_ref.shape[0]

    def rows(place):
        return out_hbm.at[pl.ds(pl.multiple_of(half * place, half), half)]

    load = pltpu.make_async_copy(own_hbm, own, sems.at[0])
    load.start()
    other = pltpu.make_async_copy(other_ref, rows(1 - low[0]), sems.at[1])
    other.start()
    load.wait()
    store = pltpu.make_async_copy(own, rows(low[0]), sems.at[2])
    store.start()
    other.wait()
    store.wait()


def rotate_kernel(x_ref, r_ref, out_ref, gathered):
    @pl.when(pl.program_id(0) == 0)
    def _():
        for z in range(Z):
            gathered[:, 128 * z : 128 * (z + 1)] = x_ref[z]

    pieces = []
    for block in range(TILE // 128):
        for piece in (0, 2, 1, 3):
            first = 128 * block + 32 * piece
            pieces.append(r_ref[first : first + 32, :])
    product = lax.dot_general(
        jnp.concatenate(pieces, axis=0),
        gathered[...],
        (((1,), (1,)), ((), ())),
        preferred_element_type=F32,
    )
    out_ref[...] = product.T[:CAP].astype(BF16)


def per_device(start_bands, hamiltonian, neighbours, basis_count, owner_rows, rotation):
    elem_size = lax.axis_size("elem")
    near = [[i, i + 1] for i in range(0, elem_size, 2)]
    far = [(i, (i + 1 if i % 2 else i - 1) % elem_size) for i in range(elem_size)]
    parity = (lax.axis_index("elem") % 2).astype(jnp.int32).reshape(1)
    second = jnp.broadcast_to((1 - parity).astype(F32)[:, None], (1, ROWS))
    low = lax.axis_index("yl").astype(jnp.int32).reshape(1)
    quad = (lax.axis_index("yl") * 2 + lax.axis_index("c")).astype(jnp.int32).reshape(1)

    columns = rotation.T

    block_bf16 = jax.ShapeDtypeStruct((BANDS_DEV, ROWS), BF16)
    block_f32 = jax.ShapeDtypeStruct((BANDS_DEV, ROWS), F32)
    current = pl.pallas_call(
        mask_kernel,
        out_shape=block_bf16,
        in_specs=[HBM, HBM],
        out_specs=VMEM,
        scratch_shapes=[
            pltpu.SMEM(basis_count.shape, jnp.int32),
            pltpu.VMEM(start_bands.shape, BF16),
            pltpu.SemaphoreType.DMA((2,)),
        ],
        compiler_params=params(8),
        cost_estimate=COST,
        name="mask",
    )(in_hbm(basis_count), in_hbm(start_bands))
    earlier = None
    for step in range(DEGREE):
        scale = 0.5 if step == 0 else 1.0
        previous = [] if earlier is None else [earlier]
        from_far = lax.ppermute(current, "elem", far)
        pair = lax.all_gather(current, "elem", axis=0, tiled=True, axis_index_groups=near)
        if step == 0:
            other_columns = lax.ppermute(columns, "yl", [(0, 1), (1, 0)])
            other_columns, pair = lax.optimization_barrier((other_columns, pair))
            pieces = pl.pallas_call(
                join_kernel,
                out_shape=jax.ShapeDtypeStruct((2 * BANDS_DEV, columns.shape[1]), BF16),
                in_specs=[SMEM, HBM, VMEM],
                out_specs=HBM,
                scratch_shapes=[
                    pltpu.VMEM(columns.shape, BF16),
                    pltpu.SemaphoreType.DMA((3,)),
                ],
                compiler_params=params(8),
                cost_estimate=COST,
                name="join",
            )(low, in_hbm(columns), other_columns)
            pieces, parity, second, quad = lax.optimization_barrier((pieces, parity, second, quad))
            rotation_all = lax.all_gather(pieces, ("z", "c"), axis=0, tiled=True)
            w_inner, w_outer = pl.pallas_call(
                couple_kernel,
                out_shape=(
                    jax.ShapeDtypeStruct((2 * ROWS, ROWS), BF16),
                    jax.ShapeDtypeStruct((ROWS, ROWS), BF16),
                ),
                in_specs=[HBM, HBM, SMEM, HBM],
                out_specs=(VMEM, VMEM),
                scratch_shapes=[
                pltpu.VMEM((ROWS, NB), F32),
                pltpu.VMEM(hamiltonian.shape, BF16),
                pltpu.SMEM(neighbours.shape, jnp.int32),
                pltpu.SMEM(basis_count.shape, jnp.int32),
                pltpu.SemaphoreType.DMA((ELEMS_DEV + 2,)),
            ],
                compiler_params=params(12),
                name="couple",
            )(in_hbm(neighbours), in_hbm(basis_count), parity, in_hbm(hamiltonian))
        partial = pl.pallas_call(
            lambda *refs, scale=scale, has_prev=bool(previous): inside_kernel(
                scale, has_prev, *refs
            ),
            out_shape=block_f32,
            in_specs=[VMEM] * (4 + len(previous)),
            out_specs=VMEM,
            compiler_params=params(8),
            cost_estimate=COST,
            name="inside",
        )(current, pair, second, *previous, w_inner)
        following = pl.pallas_call(
            lambda *refs, scale=scale: outside_kernel(scale, *refs),
            out_shape=block_bf16,
            in_specs=[VMEM] * 3,
            out_specs=VMEM,
            compiler_params=params(8),
            cost_estimate=COST,
            name="outside",
        )(partial, from_far, w_outer)
        earlier, current = current, following

    bands_quad = lax.all_gather(current, ("yl", "c"), axis=0, tiled=True)
    sent, filtered = pl.pallas_call(
        pick_kernel,
        out_shape=(jax.ShapeDtypeStruct((Z, CAP_PAD, QUAD * BANDS_DEV), BF16), block_bf16),
        in_specs=[SMEM, SMEM, VMEM],
        out_specs=(VMEM, VMEM),
        scratch_shapes=[pltpu.VMEM((ROWS + 48, QUAD * BANDS_DEV), F32)],
        compiler_params=params(8),
        cost_estimate=COST,
        name="pick",
    )(owner_rows, quad, bands_quad)
    received = lax.all_to_all(sent, "z", split_axis=0, concat_axis=0, tiled=True)
    rotated = pl.pallas_call(
        rotate_kernel,
        out_shape=jax.ShapeDtypeStruct((CAP, rotation_all.shape[1]), BF16),
        grid=(rotation_all.shape[0] // TILE,),
        in_specs=[
            pl.BlockSpec(received.shape, lambda n: (0, 0, 0)),
            pl.BlockSpec((TILE, rotation_all.shape[1]), lambda n: (n, 0)),
        ],
        out_specs=pl.BlockSpec((CAP, TILE), lambda n: (0, n)),
        scratch_shapes=[pltpu.VMEM((CAP_PAD, rotation_all.shape[1]), BF16)],
        compiler_params=params(24),
        name="rotate",
    )(received, in_hbm(rotation_all))
    return filtered, rotated


def solution(mesh):
    fine = Mesh(mesh.devices.reshape(mesh.shape["elem"], Z, 2, 2), ("elem",) + BAND_AXES)
    placed = (
        P(BAND_AXES, "elem"),
        P("elem", None, None, None),
        P("elem", None),
        P("elem"),
        P(),
        P(None, BAND_AXES),
    )
    return jax.shard_map(
        per_device,
        mesh=fine,
        in_specs=placed,
        out_specs=(P(BAND_AXES, "elem"), P(("elem",) + BAND_AXES, None)),
        check_vma=False,
    )
```

```python
import jax
import jax.numpy as jnp
from jax import lax
from jax.experimental import pallas as pl
from jax.experimental.pallas import tpu as pltpu
from jax.sharding import Mesh
from jax.sharding import PartitionSpec as P


DEGREE = 8
NB = 192
ELEMS_DEV = 4
ROWS = ELEMS_DEV * NB
BANDS_DEV = 32
CAP = 36
CAP_PAD = 40
Z = 16
QUAD = 4
BF16 = jnp.bfloat16
F32 = jnp.float32
TILE = 1024
BAND_AXES = ("z", "yl", "c")

COST = pl.CostEstimate(flops=3 * 10**8, bytes_accessed=3 << 20, transcendentals=0)
VMEM = pl.BlockSpec(memory_space=pltpu.VMEM)
SMEM = pl.BlockSpec(memory_space=pltpu.SMEM)
HBM = pl.BlockSpec(memory_space=pltpu.HBM)


def in_hbm(value):
    return pltpu.with_memory_space_constraint(value, pltpu.HBM)


def params(mib):
    return pltpu.CompilerParams(vmem_limit_bytes=mib << 20)


def lanes(i):
    return slice(NB * i, NB * (i + 1))


def column_mask(count, rows):
    return lax.broadcasted_iota(jnp.int32, (rows, NB), 1) < count


def mask_kernel(counts_hbm, start_hbm, y_ref, counts, start, sems):
    small = pltpu.make_async_copy(counts_hbm, counts, sems.at[0])
    large = pltpu.make_async_copy(start_hbm, start, sems.at[1])
    small.start()
    large.start()
    small.wait()
    large.wait()
    for i in range(ELEMS_DEV):
        block = start[:, lanes(i)]
        y_ref[:, lanes(i)] = jnp.where(
            column_mask(counts[i], BANDS_DEV), block, jnp.zeros_like(block)
        )


def couple_kernel(
    neighbours_hbm, counts_hbm, parity, h_hbm, inner_ref, outer_ref, column, h_ref, neighbours, counts, sems
):
    copies = [
        pltpu.make_async_copy(h_hbm.at[i], h_ref.at[i], sems.at[i]) for i in range(ELEMS_DEV)
    ]
    tables = [
        pltpu.make_async_copy(neighbours_hbm, neighbours, sems.at[ELEMS_DEV]),
        pltpu.make_async_copy(counts_hbm, counts, sems.at[ELEMS_DEV + 1]),
    ]
    for copy in tables + copies:
        copy.start()
    inner_ref[ROWS:, :] = jnp.zeros((ROWS, ROWS), BF16)
    outer_ref[...] = jnp.zeros_like(outer_ref)
    for copy in tables:
        copy.wait()
    slot_near = 6 - parity[0]
    slot_far = 5 + parity[0]
    for i in range(ELEMS_DEV):
        keep = column_mask(counts[i], NB)
        copies[i].wait()

        def block(slot, i=i, keep=keep):
            value = h_ref[i, slot]
            return jnp.where(keep, value, jnp.zeros_like(value))

        def rows(source):
            return pl.ds(pl.multiple_of(source * NB, NB), NB)

        column[...] = jnp.zeros_like(column)
        column[lanes(i), :] = block(0).astype(F32)
        for slot in range(1, 5):
            column[rows(neighbours[i, slot - 1]), :] += block(slot).astype(F32)
        inner_ref[:ROWS, lanes(i)] = column[...].astype(BF16)
        inner_ref[rows(ELEMS_DEV + neighbours[i, slot_near - 1]), lanes(i)] = block(slot_near)
        outer_ref[rows(neighbours[i, slot_far - 1]), lanes(i)] = block(slot_far)


def inside_kernel(scale, has_prev, y_ref, pair_ref, second_ref, *refs):
    if has_prev:
        prev_ref, w_ref, p_ref = refs
    else:
        w_ref, p_ref = refs
    near = jnp.where(
        second_ref[...] > 0.0, pair_ref[BANDS_DEV:, :].astype(F32), pair_ref[:BANDS_DEV, :].astype(F32)
    ).astype(BF16)
    total = jnp.dot(y_ref[...], w_ref[:ROWS, :], preferred_element_type=F32)
    total += jnp.dot(near, w_ref[ROWS:, :], preferred_element_type=F32)
    total = total * scale
    if has_prev:
        total = total - prev_ref[...].astype(F32)
    p_ref[...] = total


def outside_kernel(scale, p_ref, far_ref, w_ref, y_ref):
    total = jnp.dot(far_ref[...], w_ref[...], preferred_element_type=F32)
    y_ref[...] = (p_ref[...] + total * scale).astype(BF16)


def pick_kernel(owner_rows, quad, y_ref, out_ref, own_hbm, turned, sem):
    mine = pl.ds(pl.multiple_of(BANDS_DEV * quad[0], BANDS_DEV), BANDS_DEV)
    store = pltpu.make_async_copy(y_ref.at[mine], own_hbm, sem)
    store.start()
    for block in range(ROWS // 128):
        part = y_ref[:, 128 * block : 128 * (block + 1)].astype(F32)
        turned[128 * block : 128 * (block + 1), :] = part.T
    slot = lax.broadcasted_iota(jnp.int32, (CAP_PAD, QUAD * BANDS_DEV), 0)
    first = jnp.int32(0)
    for z in range(Z):
        counts = [owner_rows[QUAD * z + q] for q in range(QUAD)]
        start, count = first, counts[0]
        for q in range(1, QUAD):
            first = first + counts[q - 1]
            start = jnp.where(quad[0] == q, first, start)
            count = jnp.where(quad[0] == q, counts[q], count)
        first = first + counts[QUAD - 1]
        rows = turned[pl.ds(start, CAP_PAD), :]
        out_ref[z] = jnp.where(slot < count, rows, 0.0).astype(BF16)
    store.wait()


def join_kernel(low, own_hbm, other_ref, out_hbm, own, sems):
    half = other_ref.shape[0]

    def rows(place):
        return out_hbm.at[pl.ds(pl.multiple_of(half * place, half), half)]

    load = pltpu.make_async_copy(own_hbm, own, sems.at[0])
    load.start()
    other = pltpu.make_async_copy(other_ref, rows(1 - low[0]), sems.at[1])
    other.start()
    load.wait()
    store = pltpu.make_async_copy(own, rows(low[0]), sems.at[2])
    store.start()
    other.wait()
    store.wait()


def rotate_kernel(x_ref, r_ref, out_ref, gathered):
    @pl.when(pl.program_id(0) == 0)
    def _():
        for z in range(Z):
            gathered[:, 128 * z : 128 * (z + 1)] = x_ref[z]

    pieces = []
    for block in range(TILE // 128):
        for piece in (0, 2, 1, 3):
            first = 128 * block + 32 * piece
            pieces.append(r_ref[first : first + 32, :])
    product = lax.dot_general(
        jnp.concatenate(pieces, axis=0),
        gathered[...],
        (((1,), (1,)), ((), ())),
        preferred_element_type=F32,
    )
    out_ref[...] = product.T[:CAP].astype(BF16)


def per_device(start_bands, hamiltonian, neighbours, basis_count, owner_rows, rotation):
    elem_size = lax.axis_size("elem")
    near = [[i, i + 1] for i in range(0, elem_size, 2)]
    far = [(i, (i + 1 if i % 2 else i - 1) % elem_size) for i in range(elem_size)]
    parity = (lax.axis_index("elem") % 2).astype(jnp.int32).reshape(1)
    second = jnp.broadcast_to((1 - parity).astype(F32)[:, None], (1, ROWS))
    low = lax.axis_index("yl").astype(jnp.int32).reshape(1)
    quad = (lax.axis_index("yl") * 2 + lax.axis_index("c")).astype(jnp.int32).reshape(1)

    columns = rotation.T

    block_bf16 = jax.ShapeDtypeStruct((BANDS_DEV, ROWS), BF16)
    block_f32 = jax.ShapeDtypeStruct((BANDS_DEV, ROWS), F32)
    current = pl.pallas_call(
        mask_kernel,
        out_shape=block_bf16,
        in_specs=[HBM, HBM],
        out_specs=VMEM,
        scratch_shapes=[
            pltpu.SMEM(basis_count.shape, jnp.int32),
            pltpu.VMEM(start_bands.shape, BF16),
            pltpu.SemaphoreType.DMA((2,)),
        ],
        compiler_params=params(8),
        cost_estimate=COST,
        name="mask",
    )(in_hbm(basis_count), in_hbm(start_bands))
    earlier = None
    for step in range(DEGREE):
        scale = 0.5 if step == 0 else 1.0
        previous = [] if earlier is None else [earlier]
        from_far = lax.ppermute(current, "elem", far)
        pair = lax.all_gather(current, "elem", axis=0, tiled=True, axis_index_groups=near)
        if step == 0:
            other_columns = lax.ppermute(columns, "yl", [(0, 1), (1, 0)])
            other_columns, pair = lax.optimization_barrier((other_columns, pair))
            pieces = pl.pallas_call(
                join_kernel,
                out_shape=jax.ShapeDtypeStruct((2 * BANDS_DEV, columns.shape[1]), BF16),
                in_specs=[SMEM, HBM, VMEM],
                out_specs=HBM,
                scratch_shapes=[
                    pltpu.VMEM(columns.shape, BF16),
                    pltpu.SemaphoreType.DMA((3,)),
                ],
                compiler_params=params(8),
                cost_estimate=COST,
                name="join",
            )(low, in_hbm(columns), other_columns)
            pieces, parity, second, quad = lax.optimization_barrier((pieces, parity, second, quad))
            rotation_all = lax.all_gather(pieces, ("z", "c"), axis=0, tiled=True)
            w_inner, w_outer = pl.pallas_call(
                couple_kernel,
                out_shape=(
                    jax.ShapeDtypeStruct((2 * ROWS, ROWS), BF16),
                    jax.ShapeDtypeStruct((ROWS, ROWS), BF16),
                ),
                in_specs=[HBM, HBM, SMEM, HBM],
                out_specs=(VMEM, VMEM),
                scratch_shapes=[
                pltpu.VMEM((ROWS, NB), F32),
                pltpu.VMEM(hamiltonian.shape, BF16),
                pltpu.SMEM(neighbours.shape, jnp.int32),
                pltpu.SMEM(basis_count.shape, jnp.int32),
                pltpu.SemaphoreType.DMA((ELEMS_DEV + 2,)),
            ],
                compiler_params=params(12),
                name="couple",
            )(in_hbm(neighbours), in_hbm(basis_count), parity, in_hbm(hamiltonian))
        partial = pl.pallas_call(
            lambda *refs, scale=scale, has_prev=bool(previous): inside_kernel(
                scale, has_prev, *refs
            ),
            out_shape=block_f32,
            in_specs=[VMEM] * (4 + len(previous)),
            out_specs=VMEM,
            compiler_params=params(8),
            cost_estimate=COST,
            name="inside",
        )(current, pair, second, *previous, w_inner)
        following = pl.pallas_call(
            lambda *refs, scale=scale: outside_kernel(scale, *refs),
            out_shape=block_bf16,
            in_specs=[VMEM] * 3,
            out_specs=VMEM,
            compiler_params=params(8),
            cost_estimate=COST,
            name="outside",
        )(partial, from_far, w_outer)
        earlier, current = current, following

    bands_quad = lax.all_gather(current, ("yl", "c"), axis=0, tiled=True)
    sent, filtered = pl.pallas_call(
        pick_kernel,
        out_shape=(jax.ShapeDtypeStruct((Z, CAP_PAD, QUAD * BANDS_DEV), BF16), block_bf16),
        in_specs=[SMEM, SMEM, VMEM],
        out_specs=(VMEM, HBM),
        scratch_shapes=[
            pltpu.VMEM((ROWS + 48, QUAD * BANDS_DEV), F32),
            pltpu.SemaphoreType.DMA,
        ],
        compiler_params=params(8),
        cost_estimate=COST,
        name="pick",
    )(owner_rows, quad, bands_quad)
    received = lax.all_to_all(sent, "z", split_axis=0, concat_axis=0, tiled=True)
    rotated = pl.pallas_call(
        rotate_kernel,
        out_shape=jax.ShapeDtypeStruct((CAP, rotation_all.shape[1]), BF16),
        grid=(rotation_all.shape[0] // TILE,),
        in_specs=[
            pl.BlockSpec(received.shape, lambda n: (0, 0, 0)),
            pl.BlockSpec((TILE, rotation_all.shape[1]), lambda n: (n, 0)),
        ],
        out_specs=pl.BlockSpec((CAP, TILE), lambda n: (0, n)),
        scratch_shapes=[pltpu.VMEM((CAP_PAD, rotation_all.shape[1]), BF16)],
        compiler_params=params(24),
        name="rotate",
    )(received, in_hbm(rotation_all))
    return filtered, rotated


def solution(mesh):
    fine = Mesh(mesh.devices.reshape(mesh.shape["elem"], Z, 2, 2), ("elem",) + BAND_AXES)
    placed = (
        P(BAND_AXES, "elem"),
        P("elem", None, None, None),
        P("elem", None),
        P("elem"),
        P(),
        P(None, BAND_AXES),
    )
    return jax.shard_map(
        per_device,
        mesh=fine,
        in_specs=placed,
        out_specs=(P(BAND_AXES, "elem"), P(("elem",) + BAND_AXES, None)),
        check_vma=False,
    )
```

```python
import jax
import jax.numpy as jnp
from jax import lax
from jax.experimental import pallas as pl
from jax.experimental.pallas import tpu as pltpu
from jax.sharding import Mesh
from jax.sharding import PartitionSpec as P


DEGREE = 8
NB = 192
ELEMS_DEV = 4
ROWS = ELEMS_DEV * NB
BANDS_DEV = 32
CAP = 36
CAP_PAD = 40
Z = 16
QUAD = 4
BF16 = jnp.bfloat16
F32 = jnp.float32
TILE = 1024
BAND_AXES = ("z", "yl", "c")

COST = pl.CostEstimate(flops=3 * 10**8, bytes_accessed=3 << 20, transcendentals=0)
VMEM = pl.BlockSpec(memory_space=pltpu.VMEM)
SMEM = pl.BlockSpec(memory_space=pltpu.SMEM)
HBM = pl.BlockSpec(memory_space=pltpu.HBM)


def in_hbm(value):
    return pltpu.with_memory_space_constraint(value, pltpu.HBM)


def params(mib):
    return pltpu.CompilerParams(vmem_limit_bytes=mib << 20)


def lanes(i):
    return slice(NB * i, NB * (i + 1))


def column_mask(count, rows):
    return lax.broadcasted_iota(jnp.int32, (rows, NB), 1) < count


def mask_kernel(counts_hbm, start_hbm, y_ref, counts, start, sems):
    small = pltpu.make_async_copy(counts_hbm, counts, sems.at[0])
    large = pltpu.make_async_copy(start_hbm, start, sems.at[1])
    small.start()
    large.start()
    small.wait()
    large.wait()
    for i in range(ELEMS_DEV):
        block = start[:, lanes(i)]
        y_ref[:, lanes(i)] = jnp.where(
            column_mask(counts[i], BANDS_DEV), block, jnp.zeros_like(block)
        )


def couple_kernel(
    neighbours_hbm, counts_hbm, parity, h_hbm, inner_ref, outer_ref, column, h_ref, neighbours, counts, sems
):
    copies = [
        pltpu.make_async_copy(h_hbm.at[i], h_ref.at[i], sems.at[i]) for i in range(ELEMS_DEV)
    ]
    tables = [
        pltpu.make_async_copy(neighbours_hbm, neighbours, sems.at[ELEMS_DEV]),
        pltpu.make_async_copy(counts_hbm, counts, sems.at[ELEMS_DEV + 1]),
    ]
    for copy in tables + copies:
        copy.start()
    inner_ref[ROWS:, :] = jnp.zeros((ROWS, ROWS), BF16)
    outer_ref[...] = jnp.zeros_like(outer_ref)
    for copy in tables:
        copy.wait()
    slot_near = 6 - parity[0]
    slot_far = 5 + parity[0]
    for i in range(ELEMS_DEV):
        keep = column_mask(counts[i], NB)
        copies[i].wait()

        def block(slot, i=i, keep=keep):
            value = h_ref[i, slot]
            return jnp.where(keep, value, jnp.zeros_like(value))

        def rows(source):
            return pl.ds(pl.multiple_of(source * NB, NB), NB)

        column[...] = jnp.zeros_like(column)
        column[lanes(i), :] = block(0).astype(F32)
        for slot in range(1, 5):
            column[rows(neighbours[i, slot - 1]), :] += block(slot).astype(F32)
        inner_ref[:ROWS, lanes(i)] = column[...].astype(BF16)
        inner_ref[rows(ELEMS_DEV + neighbours[i, slot_near - 1]), lanes(i)] = block(slot_near)
        outer_ref[rows(neighbours[i, slot_far - 1]), lanes(i)] = block(slot_far)


def inside_kernel(scale, has_prev, y_ref, pair_ref, second_ref, *refs):
    if has_prev:
        prev_ref, w_ref, p_ref = refs
    else:
        w_ref, p_ref = refs
    near = jnp.where(
        second_ref[...] > 0.0, pair_ref[BANDS_DEV:, :].astype(F32), pair_ref[:BANDS_DEV, :].astype(F32)
    ).astype(BF16)
    total = jnp.dot(y_ref[...], w_ref[:ROWS, :], preferred_element_type=F32)
    total += jnp.dot(near, w_ref[ROWS:, :], preferred_element_type=F32)
    total = total * scale
    if has_prev:
        total = total - prev_ref[...].astype(F32)
    p_ref[...] = total


def outside_kernel(scale, p_ref, far_ref, w_ref, y_ref):
    total = jnp.dot(far_ref[...], w_ref[...], preferred_element_type=F32)
    y_ref[...] = (p_ref[...] + total * scale).astype(BF16)


def pick_kernel(owner_rows, quad, y_ref, out_ref, turned):
    for block in range(ROWS // 128):
        part = y_ref[:, 128 * block : 128 * (block + 1)].astype(F32)
        turned[128 * block : 128 * (block + 1), :] = part.T
    slot = lax.broadcasted_iota(jnp.int32, (CAP_PAD, QUAD * BANDS_DEV), 0)
    first = jnp.int32(0)
    for z in range(Z):
        counts = [owner_rows[QUAD * z + q] for q in range(QUAD)]
        start, count = first, counts[0]
        for q in range(1, QUAD):
            first = first + counts[q - 1]
            start = jnp.where(quad[0] == q, first, start)
            count = jnp.where(quad[0] == q, counts[q], count)
        first = first + counts[QUAD - 1]
        rows = turned[pl.ds(start, CAP_PAD), :]
        out_ref[z] = jnp.where(slot < count, rows, 0.0).astype(BF16)


def join_kernel(low, own_hbm, other_ref, out_hbm, own, sems):
    half = other_ref.shape[0]

    def rows(place):
        return out_hbm.at[pl.ds(pl.multiple_of(half * place, half), half)]

    load = pltpu.make_async_copy(own_hbm, own, sems.at[0])
    load.start()
    other = pltpu.make_async_copy(other_ref, rows(1 - low[0]), sems.at[1])
    other.start()
    load.wait()
    store = pltpu.make_async_copy(own, rows(low[0]), sems.at[2])
    store.start()
    other.wait()
    store.wait()


def rotate_kernel(x_ref, y_ref, r_ref, out_ref, filtered_hbm, gathered, sem):
    store = pltpu.make_async_copy(y_ref, filtered_hbm, sem)

    @pl.when(pl.program_id(0) == 0)
    def _():
        store.start()
        for z in range(Z):
            gathered[:, 128 * z : 128 * (z + 1)] = x_ref[z]

    pieces = []
    for block in range(TILE // 128):
        for piece in (0, 2, 1, 3):
            first = 128 * block + 32 * piece
            pieces.append(r_ref[first : first + 32, :])
    product = lax.dot_general(
        jnp.concatenate(pieces, axis=0),
        gathered[...],
        (((1,), (1,)), ((), ())),
        preferred_element_type=F32,
    )
    out_ref[...] = product.T[:CAP].astype(BF16)

    @pl.when(pl.program_id(0) == pl.num_programs(0) - 1)
    def _():
        store.wait()


def per_device(start_bands, hamiltonian, neighbours, basis_count, owner_rows, rotation):
    elem_size = lax.axis_size("elem")
    near = [[i, i + 1] for i in range(0, elem_size, 2)]
    far = [(i, (i + 1 if i % 2 else i - 1) % elem_size) for i in range(elem_size)]
    parity = (lax.axis_index("elem") % 2).astype(jnp.int32).reshape(1)
    second = jnp.broadcast_to((1 - parity).astype(F32)[:, None], (1, ROWS))
    low = lax.axis_index("yl").astype(jnp.int32).reshape(1)
    quad = (lax.axis_index("yl") * 2 + lax.axis_index("c")).astype(jnp.int32).reshape(1)

    columns = rotation.T

    block_bf16 = jax.ShapeDtypeStruct((BANDS_DEV, ROWS), BF16)
    block_f32 = jax.ShapeDtypeStruct((BANDS_DEV, ROWS), F32)
    current = pl.pallas_call(
        mask_kernel,
        out_shape=block_bf16,
        in_specs=[HBM, HBM],
        out_specs=VMEM,
        scratch_shapes=[
            pltpu.SMEM(basis_count.shape, jnp.int32),
            pltpu.VMEM(start_bands.shape, BF16),
            pltpu.SemaphoreType.DMA((2,)),
        ],
        compiler_params=params(8),
        cost_estimate=COST,
        name="mask",
    )(in_hbm(basis_count), in_hbm(start_bands))
    earlier = None
    for step in range(DEGREE):
        scale = 0.5 if step == 0 else 1.0
        previous = [] if earlier is None else [earlier]
        from_far = lax.ppermute(current, "elem", far)
        pair = lax.all_gather(current, "elem", axis=0, tiled=True, axis_index_groups=near)
        if step == 0:
            other_columns = lax.ppermute(columns, "yl", [(0, 1), (1, 0)])
            other_columns, pair = lax.optimization_barrier((other_columns, pair))
            pieces = pl.pallas_call(
                join_kernel,
                out_shape=jax.ShapeDtypeStruct((2 * BANDS_DEV, columns.shape[1]), BF16),
                in_specs=[SMEM, HBM, VMEM],
                out_specs=HBM,
                scratch_shapes=[
                    pltpu.VMEM(columns.shape, BF16),
                    pltpu.SemaphoreType.DMA((3,)),
                ],
                compiler_params=params(8),
                cost_estimate=COST,
                name="join",
            )(low, in_hbm(columns), other_columns)
            pieces, parity, second, quad = lax.optimization_barrier((pieces, parity, second, quad))
            rotation_all = lax.all_gather(pieces, ("z", "c"), axis=0, tiled=True)
            w_inner, w_outer = pl.pallas_call(
                couple_kernel,
                out_shape=(
                    jax.ShapeDtypeStruct((2 * ROWS, ROWS), BF16),
                    jax.ShapeDtypeStruct((ROWS, ROWS), BF16),
                ),
                in_specs=[HBM, HBM, SMEM, HBM],
                out_specs=(VMEM, VMEM),
                scratch_shapes=[
                pltpu.VMEM((ROWS, NB), F32),
                pltpu.VMEM(hamiltonian.shape, BF16),
                pltpu.SMEM(neighbours.shape, jnp.int32),
                pltpu.SMEM(basis_count.shape, jnp.int32),
                pltpu.SemaphoreType.DMA((ELEMS_DEV + 2,)),
            ],
                compiler_params=params(12),
                name="couple",
            )(in_hbm(neighbours), in_hbm(basis_count), parity, in_hbm(hamiltonian))
        partial = pl.pallas_call(
            lambda *refs, scale=scale, has_prev=bool(previous): inside_kernel(
                scale, has_prev, *refs
            ),
            out_shape=block_f32,
            in_specs=[VMEM] * (4 + len(previous)),
            out_specs=VMEM,
            compiler_params=params(8),
            cost_estimate=COST,
            name="inside",
        )(current, pair, second, *previous, w_inner)
        following = pl.pallas_call(
            lambda *refs, scale=scale: outside_kernel(scale, *refs),
            out_shape=block_bf16,
            in_specs=[VMEM] * 3,
            out_specs=VMEM,
            compiler_params=params(8),
            cost_estimate=COST,
            name="outside",
        )(partial, from_far, w_outer)
        earlier, current = current, following

    bands_quad = lax.all_gather(current, ("yl", "c"), axis=0, tiled=True)
    sent = pl.pallas_call(
        pick_kernel,
        out_shape=jax.ShapeDtypeStruct((Z, CAP_PAD, QUAD * BANDS_DEV), BF16),
        in_specs=[SMEM, SMEM, VMEM],
        out_specs=VMEM,
        scratch_shapes=[pltpu.VMEM((ROWS + 48, QUAD * BANDS_DEV), F32)],
        compiler_params=params(8),
        cost_estimate=COST,
        name="pick",
    )(owner_rows, quad, bands_quad)
    received = lax.all_to_all(sent, "z", split_axis=0, concat_axis=0, tiled=True)
    rotated, filtered = pl.pallas_call(
        rotate_kernel,
        out_shape=(jax.ShapeDtypeStruct((CAP, rotation_all.shape[1]), BF16), block_bf16),
        grid=(rotation_all.shape[0] // TILE,),
        in_specs=[
            pl.BlockSpec(received.shape, lambda n: (0, 0, 0)),
            VMEM,
            pl.BlockSpec((TILE, rotation_all.shape[1]), lambda n: (n, 0)),
        ],
        out_specs=(pl.BlockSpec((CAP, TILE), lambda n: (0, n)), HBM),
        scratch_shapes=[
            pltpu.VMEM((CAP_PAD, rotation_all.shape[1]), BF16),
            pltpu.SemaphoreType.DMA,
        ],
        compiler_params=params(24),
        name="rotate",
    )(received, current, in_hbm(rotation_all))
    return filtered, rotated


def solution(mesh):
    fine = Mesh(mesh.devices.reshape(mesh.shape["elem"], Z, 2, 2), ("elem",) + BAND_AXES)
    placed = (
        P(BAND_AXES, "elem"),
        P("elem", None, None, None),
        P("elem", None),
        P("elem"),
        P(),
        P(None, BAND_AXES),
    )
    return jax.shard_map(
        per_device,
        mesh=fine,
        in_specs=placed,
        out_specs=(P(BAND_AXES, "elem"), P(("elem",) + BAND_AXES, None)),
        check_vma=False,
    )
```

```python
import jax
import jax.numpy as jnp
from jax import lax
from jax.experimental import pallas as pl
from jax.experimental.pallas import tpu as pltpu
from jax.sharding import Mesh
from jax.sharding import PartitionSpec as P


DEGREE = 8
NB = 192
ELEMS_DEV = 4
ROWS = ELEMS_DEV * NB
BANDS_DEV = 32
CAP = 36
CAP_PAD = 40
Z = 16
QUAD = 4
BF16 = jnp.bfloat16
F32 = jnp.float32
TILE = 1024
BAND_AXES = ("z", "yl", "c")

COST = pl.CostEstimate(flops=3 * 10**8, bytes_accessed=3 << 20, transcendentals=0)
VMEM = pl.BlockSpec(memory_space=pltpu.VMEM)
SMEM = pl.BlockSpec(memory_space=pltpu.SMEM)
HBM = pl.BlockSpec(memory_space=pltpu.HBM)


def in_hbm(value):
    return pltpu.with_memory_space_constraint(value, pltpu.HBM)


def params(mib):
    return pltpu.CompilerParams(vmem_limit_bytes=mib << 20)


def lanes(i):
    return slice(NB * i, NB * (i + 1))


def column_mask(count, rows):
    return lax.broadcasted_iota(jnp.int32, (rows, NB), 1) < count


def mask_kernel(counts_hbm, start_hbm, y_ref, counts, start, sems):
    small = pltpu.make_async_copy(counts_hbm, counts, sems.at[0])
    large = pltpu.make_async_copy(start_hbm, start, sems.at[1])
    small.start()
    large.start()
    small.wait()
    large.wait()
    for i in range(ELEMS_DEV):
        block = start[:, lanes(i)]
        y_ref[:, lanes(i)] = jnp.where(
            column_mask(counts[i], BANDS_DEV), block, jnp.zeros_like(block)
        )


def couple_kernel(
    neighbours_hbm, counts_hbm, parity, h_hbm, inner_ref, outer_ref, column, h_ref, neighbours, counts, sems
):
    copies = [
        pltpu.make_async_copy(h_hbm.at[i], h_ref.at[i], sems.at[i]) for i in range(ELEMS_DEV)
    ]
    tables = [
        pltpu.make_async_copy(neighbours_hbm, neighbours, sems.at[ELEMS_DEV]),
        pltpu.make_async_copy(counts_hbm, counts, sems.at[ELEMS_DEV + 1]),
    ]
    for copy in tables + copies:
        copy.start()
    inner_ref[ROWS:, :] = jnp.zeros((ROWS, ROWS), BF16)
    outer_ref[...] = jnp.zeros_like(outer_ref)
    for copy in tables:
        copy.wait()
    slot_near = 6 - parity[0]
    slot_far = 5 + parity[0]
    for i in range(ELEMS_DEV):
        keep = column_mask(counts[i], NB)
        copies[i].wait()

        def block(slot, i=i, keep=keep):
            value = h_ref[i, slot]
            return jnp.where(keep, value, jnp.zeros_like(value))

        def rows(source):
            return pl.ds(pl.multiple_of(source * NB, NB), NB)

        column[...] = jnp.zeros_like(column)
        column[lanes(i), :] = block(0).astype(F32)
        for slot in range(1, 5):
            column[rows(neighbours[i, slot - 1]), :] += block(slot).astype(F32)
        inner_ref[:ROWS, lanes(i)] = column[...].astype(BF16)
        inner_ref[rows(ELEMS_DEV + neighbours[i, slot_near - 1]), lanes(i)] = block(slot_near)
        outer_ref[rows(neighbours[i, slot_far - 1]), lanes(i)] = block(slot_far)


def inside_kernel(scale, has_prev, y_ref, pair_ref, second_ref, *refs):
    if has_prev:
        prev_ref, w_ref, p_ref = refs
    else:
        w_ref, p_ref = refs
    both = jnp.dot(pair_ref[...], w_ref[ROWS:, :], preferred_element_type=F32)
    total = jnp.dot(y_ref[...], w_ref[:ROWS, :], preferred_element_type=F32)
    total += jnp.where(second_ref[...] > 0.0, both[BANDS_DEV:], both[:BANDS_DEV])
    total = total * scale
    if has_prev:
        total = total - prev_ref[...].astype(F32)
    p_ref[...] = total


def outside_kernel(scale, p_ref, far_ref, w_ref, y_ref):
    total = jnp.dot(far_ref[...], w_ref[...], preferred_element_type=F32)
    y_ref[...] = (p_ref[...] + total * scale).astype(BF16)


def pick_kernel(owner_rows, quad, y_ref, out_ref, turned):
    for block in range(ROWS // 128):
        part = y_ref[:, 128 * block : 128 * (block + 1)].astype(F32)
        turned[128 * block : 128 * (block + 1), :] = part.T
    slot = lax.broadcasted_iota(jnp.int32, (CAP_PAD, QUAD * BANDS_DEV), 0)
    first = jnp.int32(0)
    for z in range(Z):
        counts = [owner_rows[QUAD * z + q] for q in range(QUAD)]
        start, count = first, counts[0]
        for q in range(1, QUAD):
            first = first + counts[q - 1]
            start = jnp.where(quad[0] == q, first, start)
            count = jnp.where(quad[0] == q, counts[q], count)
        first = first + counts[QUAD - 1]
        rows = turned[pl.ds(start, CAP_PAD), :]
        out_ref[z] = jnp.where(slot < count, rows, 0.0).astype(BF16)


def join_kernel(low, own_hbm, other_ref, out_hbm, own, sems):
    half = other_ref.shape[0]

    def rows(place):
        return out_hbm.at[pl.ds(pl.multiple_of(half * place, half), half)]

    load = pltpu.make_async_copy(own_hbm, own, sems.at[0])
    load.start()
    other = pltpu.make_async_copy(other_ref, rows(1 - low[0]), sems.at[1])
    other.start()
    load.wait()
    store = pltpu.make_async_copy(own, rows(low[0]), sems.at[2])
    store.start()
    other.wait()
    store.wait()


def rotate_kernel(x_ref, y_ref, r_ref, out_ref, filtered_hbm, gathered, sem):
    store = pltpu.make_async_copy(y_ref, filtered_hbm, sem)

    @pl.when(pl.program_id(0) == 0)
    def _():
        store.start()
        for z in range(Z):
            gathered[:, 128 * z : 128 * (z + 1)] = x_ref[z]

    pieces = []
    for block in range(TILE // 128):
        for piece in (0, 2, 1, 3):
            first = 128 * block + 32 * piece
            pieces.append(r_ref[first : first + 32, :])
    product = lax.dot_general(
        jnp.concatenate(pieces, axis=0),
        gathered[...],
        (((1,), (1,)), ((), ())),
        preferred_element_type=F32,
    )
    out_ref[...] = product.T[:CAP].astype(BF16)

    @pl.when(pl.program_id(0) == pl.num_programs(0) - 1)
    def _():
        store.wait()


def per_device(start_bands, hamiltonian, neighbours, basis_count, owner_rows, rotation):
    elem_size = lax.axis_size("elem")
    near = [[i, i + 1] for i in range(0, elem_size, 2)]
    far = [(i, (i + 1 if i % 2 else i - 1) % elem_size) for i in range(elem_size)]
    parity = (lax.axis_index("elem") % 2).astype(jnp.int32).reshape(1)
    second = jnp.broadcast_to((1 - parity).astype(F32)[:, None], (1, ROWS))
    low = lax.axis_index("yl").astype(jnp.int32).reshape(1)
    quad = (lax.axis_index("yl") * 2 + lax.axis_index("c")).astype(jnp.int32).reshape(1)

    columns = rotation.T

    block_bf16 = jax.ShapeDtypeStruct((BANDS_DEV, ROWS), BF16)
    block_f32 = jax.ShapeDtypeStruct((BANDS_DEV, ROWS), F32)
    current = pl.pallas_call(
        mask_kernel,
        out_shape=block_bf16,
        in_specs=[HBM, HBM],
        out_specs=VMEM,
        scratch_shapes=[
            pltpu.SMEM(basis_count.shape, jnp.int32),
            pltpu.VMEM(start_bands.shape, BF16),
            pltpu.SemaphoreType.DMA((2,)),
        ],
        compiler_params=params(8),
        cost_estimate=COST,
        name="mask",
    )(in_hbm(basis_count), in_hbm(start_bands))
    earlier = None
    for step in range(DEGREE):
        scale = 0.5 if step == 0 else 1.0
        previous = [] if earlier is None else [earlier]
        from_far = lax.ppermute(current, "elem", far)
        pair = lax.all_gather(current, "elem", axis=0, tiled=True, axis_index_groups=near)
        if step == 0:
            other_columns = lax.ppermute(columns, "yl", [(0, 1), (1, 0)])
            other_columns, pair = lax.optimization_barrier((other_columns, pair))
            pieces = pl.pallas_call(
                join_kernel,
                out_shape=jax.ShapeDtypeStruct((2 * BANDS_DEV, columns.shape[1]), BF16),
                in_specs=[SMEM, HBM, VMEM],
                out_specs=HBM,
                scratch_shapes=[
                    pltpu.VMEM(columns.shape, BF16),
                    pltpu.SemaphoreType.DMA((3,)),
                ],
                compiler_params=params(8),
                cost_estimate=COST,
                name="join",
            )(low, in_hbm(columns), other_columns)
            pieces, parity, second, quad = lax.optimization_barrier((pieces, parity, second, quad))
            rotation_all = lax.all_gather(pieces, ("z", "c"), axis=0, tiled=True)
            w_inner, w_outer = pl.pallas_call(
                couple_kernel,
                out_shape=(
                    jax.ShapeDtypeStruct((2 * ROWS, ROWS), BF16),
                    jax.ShapeDtypeStruct((ROWS, ROWS), BF16),
                ),
                in_specs=[HBM, HBM, SMEM, HBM],
                out_specs=(VMEM, VMEM),
                scratch_shapes=[
                pltpu.VMEM((ROWS, NB), F32),
                pltpu.VMEM(hamiltonian.shape, BF16),
                pltpu.SMEM(neighbours.shape, jnp.int32),
                pltpu.SMEM(basis_count.shape, jnp.int32),
                pltpu.SemaphoreType.DMA((ELEMS_DEV + 2,)),
            ],
                compiler_params=params(12),
                name="couple",
            )(in_hbm(neighbours), in_hbm(basis_count), parity, in_hbm(hamiltonian))
        partial = pl.pallas_call(
            lambda *refs, scale=scale, has_prev=bool(previous): inside_kernel(
                scale, has_prev, *refs
            ),
            out_shape=block_f32,
            in_specs=[VMEM] * (4 + len(previous)),
            out_specs=VMEM,
            compiler_params=params(8),
            cost_estimate=COST,
            name="inside",
        )(current, pair, second, *previous, w_inner)
        following = pl.pallas_call(
            lambda *refs, scale=scale: outside_kernel(scale, *refs),
            out_shape=block_bf16,
            in_specs=[VMEM] * 3,
            out_specs=VMEM,
            compiler_params=params(8),
            cost_estimate=COST,
            name="outside",
        )(partial, from_far, w_outer)
        earlier, current = current, following

    bands_quad = lax.all_gather(current, ("yl", "c"), axis=0, tiled=True)
    sent = pl.pallas_call(
        pick_kernel,
        out_shape=jax.ShapeDtypeStruct((Z, CAP_PAD, QUAD * BANDS_DEV), BF16),
        in_specs=[SMEM, SMEM, VMEM],
        out_specs=VMEM,
        scratch_shapes=[pltpu.VMEM((ROWS + 48, QUAD * BANDS_DEV), F32)],
        compiler_params=params(8),
        cost_estimate=COST,
        name="pick",
    )(owner_rows, quad, bands_quad)
    received = lax.all_to_all(sent, "z", split_axis=0, concat_axis=0, tiled=True)
    rotated, filtered = pl.pallas_call(
        rotate_kernel,
        out_shape=(jax.ShapeDtypeStruct((CAP, rotation_all.shape[1]), BF16), block_bf16),
        grid=(rotation_all.shape[0] // TILE,),
        in_specs=[
            pl.BlockSpec(received.shape, lambda n: (0, 0, 0)),
            VMEM,
            pl.BlockSpec((TILE, rotation_all.shape[1]), lambda n: (n, 0)),
        ],
        out_specs=(pl.BlockSpec((CAP, TILE), lambda n: (0, n)), HBM),
        scratch_shapes=[
            pltpu.VMEM((CAP_PAD, rotation_all.shape[1]), BF16),
            pltpu.SemaphoreType.DMA,
        ],
        compiler_params=params(24),
        name="rotate",
    )(received, current, in_hbm(rotation_all))
    return filtered, rotated


def solution(mesh):
    fine = Mesh(mesh.devices.reshape(mesh.shape["elem"], Z, 2, 2), ("elem",) + BAND_AXES)
    placed = (
        P(BAND_AXES, "elem"),
        P("elem", None, None, None),
        P("elem", None),
        P("elem"),
        P(),
        P(None, BAND_AXES),
    )
    return jax.shard_map(
        per_device,
        mesh=fine,
        in_specs=placed,
        out_specs=(P(BAND_AXES, "elem"), P(("elem",) + BAND_AXES, None)),
        check_vma=False,
    )
```
